32 devices in a mesh: clip: 2 (over x), tm: 16 (over z, y, core).
Axes of the slice: x: 2, y: 2, z: 4, core: 2. Of those that a mesh axis runs over, the one named last changes fastest.
Arguments:
- tokens: bfloat16 [32768, 512], P(('clip', 'tm')), parts along dimension 0, may hold values from -6 to 6
- qkv_weight: bfloat16 [512, 1536], replicated, may hold values from -0.25 to 0.25
- out_weight: bfloat16 [512, 1024], replicated, may hold values from -0.25 to 0.25
- conv_weight: bfloat16 [3, 3, 256, 256], replicated, may hold values from -0.125 to 0.125
- norm_gain: float32 [256], replicated, may hold values from 0.25 to 1.75
- norm_bias: float32 [256], replicated, may hold values from -3 to 3
- group_map: int32 [32], P('clip'), parts along dimension 0, may hold values from 0 to 7, as said below
- token_order: int32 [2048], P('clip'), parts along dimension 0, may hold values from 0 to 1023, each once
- valid_frames: int32 [32], P('clip'), parts along dimension 0, may hold values from 1 to 16
Outputs:
- decoded: bfloat16 [32, 32, 128, 256], P('clip', 'tm'), parts along dimension 0
The draws below stay inside these ranges and needn't reach their ends.
There are 2 independent parts, one for each index of `clip`. The reference program is written for one: setup_inputs(seed, part) draws one part's arguments, and reference() takes and returns one part's arrays. A program takes and returns all parts, laid end to end along the dimension named above; an argument that names none is the same for every part. Nothing has to cross between parts.
Inputs may be any that keep to these rules, and one draw needn't show every extreme that they name: `group_map`: never falls from one run to the next, and every group from 0 to 7 holds at least one run.
All inputs are finite; a program needn't handle non-finite values.
Results may differ from the reference program's by a relative error of at most 0.0055.
The reference program's roundings to bfloat16 on the way count: a program that leaves them out, or rounds other values in their place, can miss the bound.
Values may be sent and summed in bfloat16 or wider, within the bound.
A program may use at most 64 MiB of HBM per device.

```python
import jax
import jax.numpy as jnp
from jax import lax

D = 512
HEADS = 16
C = 256
NORM_GROUPS = 32
TIME_GROUPS = 8
TOK_DEV = 1024
TOKENS = 16384
FRAMES = 16
N_TM = 16


def draw_group_map(key, part):
    cuts = jax.random.permutation(jax.random.fold_in(key, 11), N_TM - 1)[:TIME_GROUPS - 1] + 1
    positions = jnp.arange(N_TM, dtype=jnp.int32)
    return jnp.sum((positions[:, None] >= cuts[None, :]).astype(jnp.int32), axis=1).astype(jnp.int32)


def draw_valid_frames(key, part):
    lowest = FRAMES // 3
    positions = jnp.arange(N_TM, dtype=jnp.int32)
    trend = lowest + positions * (FRAMES - lowest) // max(N_TM - 1, 1)
    spread = FRAMES // 8
    jitter = jax.random.randint(jax.random.fold_in(key, 23), (N_TM,), -spread, spread + 1)
    return jnp.clip(trend + jitter, 1, FRAMES).astype(jnp.int32)


def levels(rng, dims, split, smallest, high):
    level = 1.0
    for dim, blocks in split:
        heights = jax.random.uniform(jax.random.fold_in(jax.random.fold_in(rng, 6), dim), (blocks,), jnp.float32, smallest / len(split), high / len(split))
        level = level * jnp.repeat(jnp.exp(heights), dims[dim] // blocks).reshape((-1,) + (1,) * (len(dims) - 1 - dim))
    return level


def gaussian(rng, dims, deviation, bound, pieces=(), held_as=jnp.bfloat16):
    level = levels(rng, dims, pieces, -0.22, 0.18) if pieces else 1.0
    result = jax.random.normal(rng, dims, jnp.float32) * deviation * level
    return jnp.minimum(jnp.maximum(result, -bound), bound).astype(held_as)


def setup_inputs(seed: int = 0, part: int = 0) -> dict:
    arg_keys = jax.random.split(jax.random.key(seed), 10)
    part_keys = jax.random.split(jax.random.fold_in(arg_keys[9], part), 10)
    tokens = gaussian(part_keys[0], (TOKENS, D), 1.0, 6.0, ((0, 16),))
    qkv_weight = gaussian(arg_keys[1], (D, 3 * D), D ** -0.5, 0.25)
    out_weight = gaussian(arg_keys[2], (D, 4 * C), D ** -0.5, 0.25)
    conv_weight = gaussian(arg_keys[3], (3, 3, C, C), (9 * C) ** -0.5, 0.125)
    norm_gain = jnp.clip(1.0 + 0.15 * jax.random.normal(arg_keys[4], (C,), jnp.float32), 0.25, 1.75)
    norm_bias = gaussian(arg_keys[5], (C,), 0.5, 3.0, (), jnp.float32)
    group_map = draw_group_map(jax.random.fold_in(jax.random.fold_in(arg_keys[9], part), 71), part)
    token_order = jax.random.permutation(part_keys[7], TOK_DEV).astype(jnp.int32)
    valid_frames = draw_valid_frames(jax.random.fold_in(jax.random.fold_in(arg_keys[9], part), 71), part)
    return dict(tokens=tokens, qkv_weight=qkv_weight, out_weight=out_weight, conv_weight=conv_weight, norm_gain=norm_gain, norm_bias=norm_bias, group_map=group_map, token_order=token_order, valid_frames=valid_frames)


def reference(tokens, qkv_weight, out_weight, conv_weight, norm_gain, norm_bias, group_map, token_order, valid_frames):
    head_dim = D // HEADS
    highest = lax.Precision.HIGHEST
    spans = tokens.reshape(N_TM, TOK_DEV, D)

    def span_state(span):
        mixed = jnp.dot(span, qkv_weight, preferred_element_type=jnp.float32).astype(jnp.bfloat16)
        key_feats = jax.nn.relu(mixed[:, D:2 * D]).astype(jnp.float32).reshape(TOK_DEV, HEADS, head_dim)
        value_rows = mixed[:, 2 * D:].astype(jnp.float32).reshape(TOK_DEV, HEADS, head_dim)
        state = jnp.einsum('thk,thv->khv', key_feats, value_rows, precision=highest).reshape(head_dim, D)
        return (state, lax.optimization_barrier(jnp.sum(key_feats, axis=0)).reshape(D))
    span_states, span_sums = lax.map(span_state, spans)
    earlier = (group_map[None, :] < group_map[:, None]).astype(jnp.float32)
    prefix_states = jnp.einsum('cd,dkv->ckv', earlier, span_states, precision=highest)
    prefix_sums = jnp.dot(earlier, span_sums, precision=highest)
    inverse = jnp.argsort(token_order).astype(jnp.int32)

    def span_output(packed):
        span, state, key_total = packed
        mixed = jnp.dot(span, qkv_weight, preferred_element_type=jnp.float32).astype(jnp.bfloat16)
        query_feats = jax.nn.relu(mixed[:, :D]).astype(jnp.float32).reshape(TOK_DEV, HEADS, head_dim)
        numer = jnp.einsum('thk,khv->thv', query_feats, state.reshape(head_dim, HEADS, head_dim), precision=highest)
        denom = jnp.einsum('thk,hk->th', query_feats, key_total.reshape(HEADS, head_dim), precision=highest) + 1.0
        attended = (numer / denom[:, :, None]).reshape(TOK_DEV, D).astype(jnp.bfloat16)
        raster = jnp.take(attended, inverse, axis=0)
        return jnp.dot(raster, out_weight, preferred_element_type=jnp.float32).astype(jnp.bfloat16)
    mapped = lax.map(span_output, (spans, span_states + prefix_states, span_sums + prefix_sums))
    row_tokens = TOK_DEV // N_TM
    shuffled = mapped.reshape(N_TM, N_TM, row_tokens, 2, 2, C).transpose(0, 1, 3, 2, 4, 5)
    shuffled = shuffled.reshape(N_TM, 2 * N_TM, 2 * row_tokens, C)
    row_tile = jnp.arange(2 * N_TM, dtype=jnp.int32) // 2
    frame_ids = jnp.arange(N_TM, dtype=jnp.int32)
    frame_mask = (frame_ids[:, None] < jnp.take(valid_frames, row_tile)[None, :])[:, :, None, None]
    shuffled = jnp.where(frame_mask, shuffled, jnp.zeros((), jnp.bfloat16))
    convolved = lax.conv_general_dilated(shuffled, conv_weight, (1, 1), ((1, 1), (1, 1)), dimension_numbers=('NHWC', 'HWIO', 'NHWC'), preferred_element_type=jnp.float32)
    convolved = jnp.where(frame_mask, convolved, jnp.zeros((), jnp.float32))
    group_size = C // NORM_GROUPS
    total_count = jnp.sum(valid_frames).astype(jnp.float32) * (group_size * 4 * row_tokens)

    def group_total(field):
        return lax.optimization_barrier(jnp.sum(field, axis=(0, 1, 2))).reshape(NORM_GROUPS, group_size).sum(axis=1)
    group_mean = group_total(convolved) / total_count
    centred = jnp.where(frame_mask, convolved - jnp.repeat(group_mean, group_size), jnp.zeros((), jnp.float32))
    group_var = group_total(centred * centred) / total_count
    norm_scale = norm_gain * lax.rsqrt(jnp.repeat(group_var, group_size) + 1e-05)
    normed = centred * norm_scale + norm_bias
    decoded = jnp.where(frame_mask, jax.nn.silu(normed), jnp.zeros((), jnp.float32))
    return decoded.astype(jnp.bfloat16)
```

```python
import functools

import jax
import jax.numpy as jnp
from jax import lax
from jax.experimental import pallas as pl
from jax.experimental.pallas import tpu as pltpu
from jax.sharding import PartitionSpec as P

HEADS = 16
NORM_GROUPS = 32
MESH = pl.DeviceIdType.MESH
F32 = jnp.float32
BF16 = jnp.bfloat16
CHUNK = 256
BLOCK = 256
VMEM = 66650112


def flat(cells):
    frames, rows, width = cells.shape
    if rows % 16 == 0:
        return cells.reshape(frames * rows, width)
    return cells.astype(F32).reshape(frames * rows, width).astype(BF16)


def mega(
    n,
    tokens_hbm,
    qkv_hbm,
    out_hbm,
    conv_hbm,
    gain_ref,
    bias_ref,
    group_ref,
    order_ref,
    valid_ref,
    decoded_ref,
    tokens_ref,
    qkv_ref,
    outw_ref,
    convw_ref,
    sent_tokens,
    tile_tokens,
    state_acc,
    sum_acc,
    sent_state,
    all_state,
    all_total,
    running,
    prefix,
    rows_ref,
    cells,
    halo,
    conv_acc,
    stat_acc,
    sent_stat,
    all_stat,
    out_buf,
    load_sem,
    tok_send,
    tok_recv,
    core_send,
    core_recv,
    col_send,
    col_recv,
    row_send,
    row_recv,
    halo_send,
    halo_recv,
    stat_send,
    stat_recv,
):
    me = lax.axis_index("tm")
    count, width = tokens_ref.shape
    row_tokens = count // n
    chunks = count // CHUNK
    frames_per = CHUNK // row_tokens
    head_dim = width // HEADS
    channels = gain_ref.shape[1]
    blocks = width // BLOCK
    heads_per = BLOCK // head_dim
    group_size = channels // NORM_GROUPS

    loads = [
        pltpu.make_async_copy(a, b, load_sem.at[i])
        for i, (a, b) in enumerate(
            [
                (tokens_hbm, tokens_ref),
                (qkv_hbm, qkv_ref),
                (out_hbm, outw_ref),
                (conv_hbm, convw_ref),
            ]
        )
    ]
    for load in loads:
        load.start()

    barrier = pltpu.get_barrier_semaphore()

    @pl.loop(1, n)
    def _(s):
        pl.semaphore_signal(
            barrier, inc=1, device_id={"tm": lax.rem(me + s, n)}, device_id_type=MESH
        )

    def exchange(s, src, dst, send_sem, recv_sem):
        return pltpu.make_async_remote_copy(
            src_ref=src,
            dst_ref=dst,
            send_sem=send_sem.at[s],
            recv_sem=recv_sem.at[s],
            device_id={"tm": lax.rem(me + s, n)},
            device_id_type=MESH,
        )

    def tok_copy(t):
        return pltpu.make_async_remote_copy(
            src_ref=sent_tokens.at[t],
            dst_ref=tile_tokens.at[me],
            send_sem=tok_send.at[t],
            recv_sem=tok_recv.at[me],
            device_id={"tm": t},
            device_id_type=MESH,
        )

    def tok_arrival(t):
        return pltpu.make_async_remote_copy(
            src_ref=sent_tokens.at[t],
            dst_ref=tile_tokens.at[t],
            send_sem=tok_send.at[t],
            recv_sem=tok_recv.at[t],
            device_id={"tm": t},
            device_id_type=MESH,
        )

    levels = n // 4
    core_peer = me + 1 - 2 * lax.rem(me, 2)
    row_peer = me + 2 - 4 * lax.rem(lax.div(me, 2), 2)

    def column_copy(k):
        return pltpu.make_async_remote_copy(
            src_ref=sent_state,
            dst_ref=all_state.at[me],
            send_sem=col_send.at[k],
            recv_sem=col_recv.at[k],
            device_id={"tm": lax.rem(me + 4 * k, n)},
            device_id_type=MESH,
        )

    def pass_on(source, peer, send_sem, recv_sem):
        return pltpu.make_async_remote_copy(
            src_ref=all_state.at[source],
            dst_ref=all_state.at[source],
            send_sem=send_sem,
            recv_sem=recv_sem,
            device_id={"tm": peer},
            device_id_type=MESH,
        )

    def row_pass(k):
        source = lax.rem(me + n - 4 * k, n)
        return pass_on(source, row_peer, row_send.at[k], row_recv.at[k])

    def core_pass(k, d):
        source = lax.rem(me + d * (row_peer - me) + n - 4 * k, n)
        return pass_on(source, core_peer, core_send.at[d, k], core_recv.at[d, k])

    def stat_copy(s):
        return exchange(s, sent_stat, all_stat.at[me], stat_send, stat_recv)

    half = chunks // 2
    side = lax.div(me, n // 2)
    near = side * half
    far = half - near

    loads[0].wait()
    loads[1].wait()
    state_acc[...] = jnp.zeros_like(state_acc)
    sum_acc[...] = jnp.zeros_like(sum_acc)

    @pl.loop(0, chunks)
    def _(c):
        rows = pl.ds(pl.multiple_of(c * CHUNK, CHUNK), CHUNK)
        mixed = jnp.dot(
            tokens_ref[rows, :], qkv_ref[:, width : 3 * width], preferred_element_type=F32
        ).astype(BF16)
        keys = jnp.maximum(mixed[:, :width], jnp.zeros((), BF16))
        sum_acc[...] += keys.astype(F32).reshape(CHUNK // 8, 8, width).sum(axis=0)
        for b in range(blocks):
            lanes = slice(b * BLOCK, (b + 1) * BLOCK)
            state_acc[b] += lax.dot_general(
                keys[:, lanes],
                mixed[:, width + b * BLOCK : width + (b + 1) * BLOCK],
                (((0,), (0,)), ((), ())),
                preferred_element_type=F32,
            )

    head_row = lax.broadcasted_iota(jnp.int32, (BLOCK, BLOCK), 0) // head_dim
    head_col = lax.broadcasted_iota(jnp.int32, (BLOCK, BLOCK), 1) // head_dim
    same_head = head_row == head_col
    pieces = width // 128
    sum_at = pieces * head_dim
    for b in range(blocks):
        own = jnp.where(same_head, state_acc[b], 0.0)
        own = own.reshape(heads_per, head_dim, BLOCK).sum(axis=0).astype(BF16)
        for i in range(BLOCK // 128):
            at = (b * (BLOCK // 128) + i) * head_dim
            sent_state[at : at + head_dim, :] = own[:, i * 128 : (i + 1) * 128]
    key_sum = jnp.sum(sum_acc[...], axis=0, keepdims=True)
    high = key_sum.astype(BF16).astype(F32)
    line = lax.broadcasted_iota(jnp.int32, (16, 128), 0)
    packed = jnp.zeros((16, 128), F32)
    for i in range(pieces):
        lanes = slice(i * 128, (i + 1) * 128)
        packed = jnp.where(line == i, high[:, lanes], packed)
        packed = jnp.where(line == pieces + i, (key_sum - high)[:, lanes], packed)
    sent_state[sum_at : sum_at + 16, :] = packed.astype(BF16)

    all_state[me] = sent_state[...]
    pl.semaphore_wait(barrier, n - 1)

    @pl.loop(1, levels)
    def _(k):
        column_copy(k).start()

    row_pass(0).start()
    core_pass(0, 0).start()

    def permute(to):
        place = lax.broadcasted_iota(jnp.int32, (CHUNK, count), 0) + to * CHUNK
        pick = jnp.where(order_ref[...] == place, 1.0, 0.0).astype(BF16)
        moved = jnp.dot(pick, tokens_ref[...], preferred_element_type=F32)
        sent_tokens[pl.ds(to * frames_per, frames_per)] = moved.reshape(
            frames_per, row_tokens, width
        ).astype(BF16)

    def near_tile(k):
        return near * frames_per + lax.rem(me + k, n // 2)

    def far_tile(k):
        return far * frames_per + lax.rem(me + k, n // 2)

    @pl.loop(0, half)
    def _(k):
        permute(near + k)

    @pl.loop(1, n // 2)
    def _(k):
        tok_copy(near_tile(k)).start()

    tile_tokens[me] = sent_tokens[me]

    @pl.loop(0, half)
    def _(k):
        permute(far + k)

    @pl.loop(0, n // 2)
    def _(k):
        tok_copy(far_tile(k)).start()

    @pl.loop(1, levels)
    def _(k):
        column_copy(k).wait_recv()
        row_pass(k).start()
        core_pass(k, 0).start()

    @pl.loop(0, levels)
    def _(k):
        row_pass(k).wait_recv()
        core_pass(k, 1).start()

    def chunk_rows(c):
        return pl.ds(pl.multiple_of(c * CHUNK, CHUNK), CHUNK)

    def queries(c):
        @pl.loop(0, frames_per)
        def _(k):
            t = c * frames_per + k

            @pl.when(t != me)
            def _():
                tok_arrival(t).wait_recv()

        mixed = jnp.dot(
            flat(tile_tokens[pl.ds(c * frames_per, frames_per)]),
            qkv_ref[:, 0:width],
            preferred_element_type=F32,
        ).astype(BF16)
        rows_ref[chunk_rows(c), :] = jnp.maximum(mixed, jnp.zeros((), BF16)).astype(F32)

    @pl.loop(0, half)
    def _(k):
        queries(near + k)

    @pl.loop(0, levels)
    def _(k):
        core_pass(k, 0).wait_recv()
        core_pass(k, 1).wait_recv()

    running[...] = jnp.zeros_like(running)
    prefix[...] = jnp.zeros_like(prefix)

    @pl.loop(0, n)
    def _(f):
        new_group = group_ref[f] != group_ref[jnp.maximum(f - 1, 0)]
        before = jnp.where(new_group, running[...], prefix[...])
        prefix[...] = before
        own = all_state[f].astype(F32)
        running[...] += own
        all_total[f] = before + own

    valid_rows = valid_ref[me] * row_tokens
    loads[2].wait()

    def widen(even, odd):
        column = lax.rem(lax.broadcasted_iota(jnp.int32, even.shape, 0), row_tokens)
        odd_left = jnp.where(column == 0, 0.0, pltpu.roll(odd, 1, 0))
        even_right = jnp.where(column == row_tokens - 1, 0.0, pltpu.roll(even, CHUNK - 1, 0))
        return [x.astype(BF16) for x in (odd_left, even, odd, even_right)]

    def down_copy(c):
        rows = pl.ds(pl.multiple_of(c * CHUNK, CHUNK), CHUNK)
        return pltpu.make_async_remote_copy(
            src_ref=cells.at[1, rows, channels : 3 * channels],
            dst_ref=halo.at[0, rows, :],
            send_sem=halo_send.at[0, c],
            recv_sem=halo_recv.at[0, c],
            device_id={"tm": lax.rem(me + 1, n)},
            device_id_type=MESH,
        )

    def up_copy(c):
        rows = pl.ds(pl.multiple_of(c * CHUNK, CHUNK), CHUNK)
        return pltpu.make_async_remote_copy(
            src_ref=cells.at[0, rows, channels : 3 * channels],
            dst_ref=halo.at[1, rows, :],
            send_sem=halo_send.at[1, c],
            recv_sem=halo_recv.at[1, c],
            device_id={"tm": lax.rem(me + n - 1, n)},
            device_id_type=MESH,
        )

    head_ones = same_head.astype(F32).astype(BF16)
    reach = 3 * channels
    loads[3].wait()

    def project(c):
        rows = chunk_rows(c)

        def attend(k, carry):
            f = c * frames_per + k
            total = all_total[f]
            key_total = jnp.concatenate(
                [
                    total[sum_at + i : sum_at + i + 1, :]
                    + total[sum_at + pieces + i : sum_at + pieces + i + 1, :]
                    for i in range(pieces)
                ],
                axis=1,
            )
            here = pl.ds(pl.multiple_of(f * row_tokens, 8), row_tokens)
            query = rows_ref[here, :]
            scaled = (query * key_total).astype(BF16)
            query = query.astype(BF16)
            for b in range(blocks):
                lanes = slice(b * BLOCK, (b + 1) * BLOCK)
                first = b * (BLOCK // 128)
                state = jnp.concatenate(
                    [
                        total[i * head_dim : (i + 1) * head_dim, :]
                        for i in range(first, first + BLOCK // 128)
                    ],
                    axis=1,
                )
                high = state.astype(BF16).astype(F32)
                numer = jnp.zeros((row_tokens, BLOCK), F32)
                for part in (high, state - high):
                    spread = jnp.concatenate([part] * heads_per, axis=0)
                    spread = jnp.where(same_head, spread, 0.0).astype(BF16)
                    numer += jnp.dot(query[:, lanes], spread, preferred_element_type=F32)
                denom = jnp.dot(scaled[:, lanes], head_ones, preferred_element_type=F32) + 1.0
                rows_ref[here, lanes] = numer / denom
            return carry

        lax.fori_loop(0, frames_per, attend, 0, unroll=frames_per <= 4)
        mapped = jnp.dot(rows_ref[rows, :].astype(BF16), outw_ref[...], preferred_element_type=F32)
        row = lax.broadcasted_iota(jnp.int32, mapped.shape, 0) + c * CHUNK
        mapped = jnp.where(row < valid_rows, mapped, 0.0)
        for a in range(2):
            even = mapped[:, 2 * a * channels : (2 * a + 1) * channels]
            odd = mapped[:, (2 * a + 1) * channels : (2 * a + 2) * channels]
            for i, part in enumerate(widen(even, odd)):
                cells[a, rows, i * channels : (i + 1) * channels] = part

        @pl.when(me < n - 1)
        def _():
            down_copy(c).start()

        @pl.when(me > 0)
        def _():
            up_copy(c).start()

    def convolve(c):
        rows = chunk_rows(c)
        for r in range(2):
            for b in range(2):
                lanes = slice(b * channels, b * channels + reach)
                conv_acc[r, rows, b * channels : (b + 1) * channels] = jnp.dot(
                    cells[0, rows, lanes], convw_ref[1 - r], preferred_element_type=F32
                ) + jnp.dot(cells[1, rows, lanes], convw_ref[2 - r], preferred_element_type=F32)

    def finish(c, r):
        rows = chunk_rows(c)

        if r == 0:

            @pl.when(me > 0)
            def _():
                down_copy(c).wait_recv()

        else:

            @pl.when(me < n - 1)
            def _():
                up_copy(c).wait_recv()

        row = lax.broadcasted_iota(jnp.int32, (CHUNK, channels), 0) + c * CHUNK
        edge = halo[r, rows, :].astype(F32)
        parts = widen(edge[:, :channels], edge[:, channels:])
        results = []
        for b in range(2):
            taps = jnp.concatenate(parts[b : b + 3], axis=1)
            lanes = slice(b * channels, (b + 1) * channels)
            result = conv_acc[r, rows, lanes] + jnp.dot(
                taps, convw_ref[2 * r], preferred_element_type=F32
            )
            result = jnp.where(row < valid_rows, result, 0.0)
            results.append(result)
            for h in range(0, channels, 128):
                out_buf[r, h // 128, pl.ds(c * 2 * CHUNK + b, CHUNK, 2), :] = result[
                    :, h : h + 128
                ]
        eights = [x.reshape(CHUNK // 8, 8, channels).sum(axis=0) for x in results]
        total = jnp.sum(eights[0] + eights[1], axis=0, keepdims=True)
        size = jnp.clip(valid_rows - c * CHUNK, 0, CHUNK) * 2
        centre = total / jnp.maximum(size, 1).astype(F32)
        square = jnp.zeros((8, channels), F32)
        for x in results:
            off = jnp.where(row < valid_rows, x - centre, 0.0)
            square += (off * off).reshape(CHUNK // 8, 8, channels).sum(axis=0)
        square = jnp.sum(square, axis=0, keepdims=True)
        line = lax.broadcasted_iota(jnp.int32, (8, channels), 0)
        stat_acc[2 * c + r] = jnp.where(
            line == 0, total, jnp.where(line == 1, square, size.astype(F32))
        )

    inside = [me != n // 2, me != n // 2 - 1]

    def far_chunk(k):
        return far + k + side * (half - 1 - 2 * k)

    @pl.when(me == 0)
    def _():
        halo[0] = jnp.zeros(halo.shape[1:], BF16)

    @pl.when(me == n - 1)
    def _():
        halo[1] = jnp.zeros(halo.shape[1:], BF16)

    @pl.loop(0, half)
    def _(k):
        project(near + k)

    @pl.loop(0, half)
    def _(k):
        convolve(near + k)

    @pl.loop(0, half)
    def _(k):
        c = far_chunk(k)
        queries(c)
        project(c)
        convolve(c)

        for r in range(2):

            @pl.when(inside[r])
            def _():
                finish(jnp.where(k == 0, near, far_chunk(k - 1)), r)

                @pl.when(k == 0)
                def _():
                    finish(near + 1, r)

    for r in range(2):

        @pl.when(inside[r])
        def _():
            finish(far_chunk(half - 1), r)

        @pl.when(jnp.logical_not(inside[r]))
        def _():
            @pl.loop(0, half)
            def _(k):
                finish(far + k, r)

            @pl.loop(0, half)
            def _(k):
                finish(near + k + (1 - side) * (half - 1 - 2 * k), r)

    group_row = lax.broadcasted_iota(jnp.int32, (channels, channels), 0) // group_size
    group_col = lax.broadcasted_iota(jnp.int32, (channels, channels), 1) // group_size
    group_ones = jnp.where(group_row == group_col, 1.0, 0.0).astype(BF16)

    def group_total(sums):
        parts = []
        for _ in range(3):
            part = sums.astype(BF16)
            parts.append(part)
            sums = sums - part.astype(F32)
        line = lax.broadcasted_iota(jnp.int32, (16, channels), 0)
        stacked = jnp.zeros((16, channels), F32)
        for i, part in enumerate(parts):
            stacked = jnp.where(line == i, part.astype(F32), stacked)
        found = jnp.dot(stacked.astype(BF16), group_ones, preferred_element_type=F32)
        return found[0:1] + found[1:2] + found[2:3]

    def combine(field):
        total, square, size = [field[:, i, :] for i in range(3)]
        whole = jnp.sum(size, axis=0, keepdims=True)
        mean = jnp.sum(total, axis=0, keepdims=True) / whole
        off = total / jnp.maximum(size, 1.0) - mean
        return mean, jnp.sum(square + size * (off * off), axis=0, keepdims=True), whole

    mean, square, whole = combine(stat_acc)
    line = lax.broadcasted_iota(jnp.int32, (8, channels), 0)
    sent_stat[...] = jnp.where(line == 0, mean * whole, jnp.where(line == 1, square, whole))

    @pl.loop(1, n)
    def _(s):
        stat_copy(s).start()

    all_stat[me] = sent_stat[...]

    @pl.loop(1, n)
    def _(s):
        stat_copy(s).wait_recv()

    mean, square, whole = combine(all_stat)
    group_mean = group_total(mean) / group_size
    off = mean - group_mean
    group_square = group_total(square + whole * (off * off))
    mean = group_mean
    scale = gain_ref[...] * lax.rsqrt(group_square / (whole * group_size) + 1e-05)
    sides = [(r, h) for r in range(2) for h in range(channels // 128)]
    half_scale = 0.5 * scale
    half_shift = 0.5 * (bias_ref[...] - mean * scale)

    @pl.loop(0, n)
    def _(f):
        pixels = pl.ds(pl.multiple_of(f * 2 * row_tokens, 8), 2 * row_tokens)
        live = f < valid_ref[me]
        for r, h in sides:
            lanes = slice(h * 128, (h + 1) * 128)
            normed = out_buf[r, h, pixels, :] * half_scale[:, lanes] + half_shift[:, lanes]
            silu = normed + normed * jnp.tanh(normed)
            decoded_ref[f, r, :, lanes] = jnp.where(live, silu, 0.0).astype(BF16)

    @pl.loop(0, chunks)
    def _(c):
        @pl.when(me < n - 1)
        def _():
            down_copy(c).wait_send()

        @pl.when(me > 0)
        def _():
            up_copy(c).wait_send()

    @pl.loop(1, n)
    def _(s):
        tok_copy(lax.rem(me + s, n)).wait_send()
        stat_copy(s).wait_send()

    @pl.loop(1, levels)
    def _(k):
        column_copy(k).wait_send()

    @pl.loop(0, levels)
    def _(k):
        row_pass(k).wait_send()
        core_pass(k, 0).wait_send()
        core_pass(k, 1).wait_send()


def local(
    tokens,
    qkv_weight,
    out_weight,
    conv_weight,
    norm_gain,
    norm_bias,
    group_map,
    token_order,
    valid_frames,
):
    n = lax.axis_size("tm")
    count, width = tokens.shape
    channels = conv_weight.shape[3]
    row_tokens = count // n
    chunks = count // CHUNK
    state_shape = (width // 128 * (width // HEADS) + 16, 128)
    anywhere = pl.BlockSpec(memory_space=pltpu.HBM)
    vmem = pl.BlockSpec(memory_space=pltpu.VMEM)
    smem = pl.BlockSpec(memory_space=pltpu.SMEM)
    dma = pltpu.SemaphoreType.DMA
    return pl.pallas_call(
        functools.partial(mega, n),
        out_shape=pltpu.VMEM((n, 2, 2 * row_tokens, channels), BF16),
        in_specs=[anywhere] * 4 + [vmem, vmem, smem, vmem, smem],
        out_specs=vmem,
        scratch_shapes=[
            pltpu.VMEM((count, width), BF16),
            pltpu.VMEM((width, 3 * width), BF16),
            pltpu.VMEM((width, 4 * channels), BF16),
            pltpu.VMEM((3, 3 * channels, channels), BF16),
            pltpu.VMEM((n, row_tokens, width), BF16),
            pltpu.VMEM((n, row_tokens, width), BF16),
            pltpu.VMEM((width // BLOCK, BLOCK, BLOCK), F32),
            pltpu.VMEM((8, width), F32),
            pltpu.VMEM(state_shape, BF16),
            pltpu.VMEM((n,) + state_shape, BF16),
            pltpu.VMEM((n,) + state_shape, F32),
            pltpu.VMEM(state_shape, F32),
            pltpu.VMEM(state_shape, F32),
            pltpu.VMEM((count, width), F32),
            pltpu.VMEM((2, count, 4 * channels), BF16),
            pltpu.VMEM((2, count, 2 * channels), BF16),
            pltpu.VMEM((2, count, 2 * channels), F32),
            pltpu.VMEM((2 * chunks, 8, channels), F32),
            pltpu.VMEM((8, channels), F32),
            pltpu.VMEM((n, 8, channels), F32),
            pltpu.VMEM((2, channels // 128, 2 * count, 128), F32),
            dma((4,)),
            dma((n,)),
            dma((n,)),
            dma((2, n // 4)),
            dma((2, n // 4)),
            dma((n // 4,)),
            dma((n // 4,)),
            dma((n // 4,)),
            dma((n // 4,)),
            dma((2, chunks)),
            dma((2, chunks)),
            dma((n,)),
            dma((n,)),
        ],
        compiler_params=pltpu.CompilerParams(
            collective_id=0, has_side_effects=True, vmem_limit_bytes=VMEM - 2 * count * 4 * channels
        ),
    )(
        tokens,
        qkv_weight,
        out_weight,
        conv_weight.reshape(3, 3 * channels, channels),
        norm_gain[None],
        norm_bias[None],
        group_map,
        token_order[None],
        valid_frames,
    )


def solution(mesh):
    in_specs = (P(("clip", "tm"), None), P(), P(), P(), P(), P(), P("clip"), P("clip"), P("clip"))
    out_specs = P("clip", "tm", None, None)
    return jax.shard_map(local, mesh=mesh, in_specs=in_specs, out_specs=out_specs, check_vma=False)
```

```python
import functools

import jax
import jax.numpy as jnp
from jax import lax
from jax.experimental import pallas as pl
from jax.experimental.pallas import tpu as pltpu
from jax.sharding import PartitionSpec as P

HEADS = 16
NORM_GROUPS = 32
MESH = pl.DeviceIdType.MESH
F32 = jnp.float32
BF16 = jnp.bfloat16
CHUNK = 256
BLOCK = 256
VMEM = 66650112


def flat(cells):
    rows, width = cells.shape[-2:]
    every = cells.size // width
    if rows % 16 == 0:
        return cells.reshape(every, width)
    return cells.astype(F32).reshape(every, width).astype(BF16)


def mega(
    n,
    tokens_hbm,
    qkv_hbm,
    out_hbm,
    conv_hbm,
    gain_ref,
    bias_ref,
    group_ref,
    order_ref,
    valid_ref,
    decoded_ref,
    tokens_ref,
    qkv_ref,
    outw_ref,
    convw_ref,
    sent_tokens,
    tile_tokens,
    state_acc,
    sum_acc,
    sent_state,
    all_state,
    all_total,
    running,
    prefix,
    rows_ref,
    made,
    near_rows,
    cells,
    stat_acc,
    sent_stat,
    all_stat,
    out_buf,
    load_sem,
    tok_send,
    tok_recv,
    core_send,
    core_recv,
    col_send,
    col_recv,
    row_send,
    row_recv,
    made_send,
    relay_send,
    near_recv,
    stat_send,
    stat_recv,
):
    me = lax.axis_index("tm")
    count, width = tokens_ref.shape
    row_tokens = count // n
    pair_tokens = 2 * row_tokens
    chunks = count // CHUNK
    share = n // (2 * chunks)
    head_dim = width // HEADS
    channels = gain_ref.shape[1]
    blocks = width // BLOCK
    heads_per = BLOCK // head_dim
    group_size = channels // NORM_GROUPS

    levels = n // 4
    level = lax.div(me, 4)
    y = lax.rem(lax.div(me, 2), 2)
    core = lax.rem(me, 2)
    side = lax.div(me, n // 2)
    place = lax.div(me, n // chunks)
    inward = place + side * (chunks - 1 - 2 * place)
    inner = inward == 1
    mine = 2 * level + core
    core_peer = me + 1 - 2 * core
    row_peer = me + 2 - 4 * y

    def facing(k):
        return k + side * (chunks - 1 - 2 * k)

    def frame_of(source, column):
        return 4 * lax.div(source, 2) + 2 * column + lax.rem(source, 2)

    loads = [
        pltpu.make_async_copy(a, b, load_sem.at[i])
        for i, (a, b) in enumerate(
            [
                (tokens_hbm, tokens_ref),
                (qkv_hbm, qkv_ref),
                (out_hbm, outw_ref),
                (conv_hbm, convw_ref),
            ]
        )
    ]
    for load in loads:
        load.start()

    barrier = pltpu.get_barrier_semaphore()

    @pl.loop(1, n)
    def _(s):
        pl.semaphore_signal(
            barrier, inc=1, device_id={"tm": lax.rem(me + s, n)}, device_id_type=MESH
        )

    def remote(src, dst, send_sem, recv_sem, device):
        return pltpu.make_async_remote_copy(
            src_ref=src,
            dst_ref=dst,
            send_sem=send_sem,
            recv_sem=recv_sem,
            device_id={"tm": device},
            device_id_type=MESH,
        )

    def tok_copy(slot):
        return remote(
            sent_tokens.at[slot],
            tile_tokens.at[mine],
            tok_send.at[slot],
            tok_recv.at[mine],
            4 * lax.div(slot, 2) + 2 * y + lax.rem(slot, 2),
        )

    def tok_arrival(source):
        return remote(
            sent_tokens.at[source],
            tile_tokens.at[source],
            tok_send.at[source],
            tok_recv.at[source],
            4 * lax.div(source, 2) + 2 * y + lax.rem(source, 2),
        )

    def column_copy(k):
        return remote(
            sent_state,
            all_state.at[me],
            col_send.at[k],
            col_recv.at[k],
            lax.rem(me + 4 * k, n),
        )

    def pass_on(source, peer, send_sem, recv_sem):
        return remote(all_state.at[source], all_state.at[source], send_sem, recv_sem, peer)

    def row_pass(k):
        source = lax.rem(me + n - 4 * k, n)
        return pass_on(source, row_peer, row_send.at[k], row_recv.at[k])

    def core_pass(k, d):
        source = lax.rem(me + d * (row_peer - me) + n - 4 * k, n)
        return pass_on(source, core_peer, core_send.at[d, k], core_recv.at[d, k])

    def stat_copy(s):
        return remote(
            sent_stat,
            all_stat.at[me],
            stat_send.at[s],
            stat_recv.at[s],
            lax.rem(me + s, n),
        )

    across = lax.rem(y + core, 2)
    outer_owner = 4 * level + 3 * core
    inner_owner = 4 * level + 1 + core
    beyond = 4 * level - 1 + 5 * core
    exists = jnp.logical_and(beyond >= 0, beyond < n)
    beyond_device = jnp.clip(beyond, 0, n - 1)
    far_slot = 2 * core
    peer_slot = 2 - 2 * core

    def made_copy(kind, c):
        if kind == 0:
            part, device, slot = 1 - core, inner_owner, 1
        elif kind == 1:
            part, device, slot = core, beyond_device, peer_slot
        elif kind == 2:
            part = core
            device = across * outer_owner + (1 - across) * inner_owner
            slot = across + (1 - across) * far_slot
        else:
            part, device, slot = 1 - core, 4 * level + 2 - core, far_slot
        return remote(
            made.at[part, c],
            near_rows.at[slot, c, y],
            made_send.at[kind, c],
            near_recv.at[slot, c, y],
            device,
        )

    def relay_copy(c):
        return remote(
            near_rows.at[1, c, 1 - y],
            near_rows.at[far_slot, c, 1 - y],
            relay_send.at[c],
            near_recv.at[far_slot, c, 1 - y],
            core_peer,
        )

    def near_arrival(slot, c, column):
        return remote(
            near_rows.at[slot, c, column],
            near_rows.at[slot, c, column],
            made_send.at[0, c],
            near_recv.at[slot, c, column],
            core_peer,
        )

    loads[0].wait()

    def permute(to):
        where = lax.broadcasted_iota(jnp.int32, (CHUNK, count), 0) + to * CHUNK
        pick = jnp.where(order_ref[...] == where, 1.0, 0.0).astype(BF16)
        moved = jnp.dot(pick, tokens_ref[...], preferred_element_type=F32)
        sent_tokens[pl.ds(to * share, share)] = moved.reshape(share, pair_tokens, width).astype(
            BF16
        )

    def send_tiles(to):
        @pl.loop(0, share)
        def _(k):
            slot = to * share + k

            @pl.when(slot != mine)
            def _():
                tok_copy(slot).start()

    targets = [facing(x) for x in (inward + 1, inward * 0, 2 - inward, inward * 0 + 3)]

    loads[1].wait()
    state_acc[...] = jnp.zeros_like(state_acc)
    sum_acc[...] = jnp.zeros_like(sum_acc)

    @pl.loop(0, chunks)
    def _(c):
        rows = pl.ds(pl.multiple_of(c * CHUNK, CHUNK), CHUNK)
        mixed = jnp.dot(
            tokens_ref[rows, :], qkv_ref[:, width : 3 * width], preferred_element_type=F32
        ).astype(BF16)
        keys = jnp.maximum(mixed[:, :width], jnp.zeros((), BF16))
        sum_acc[...] += keys.astype(F32).reshape(CHUNK // 8, 8, width).sum(axis=0)
        for b in range(blocks):
            lanes = slice(b * BLOCK, (b + 1) * BLOCK)
            state_acc[b] += lax.dot_general(
                keys[:, lanes],
                mixed[:, width + b * BLOCK : width + (b + 1) * BLOCK],
                (((0,), (0,)), ((), ())),
                preferred_element_type=F32,
            )

    head_row = lax.broadcasted_iota(jnp.int32, (BLOCK, BLOCK), 0) // head_dim
    head_col = lax.broadcasted_iota(jnp.int32, (BLOCK, BLOCK), 1) // head_dim
    same_head = head_row == head_col
    pieces = width // 128
    sum_at = pieces * head_dim
    for b in range(blocks):
        own = jnp.where(same_head, state_acc[b], 0.0)
        own = own.reshape(heads_per, head_dim, BLOCK).sum(axis=0).astype(BF16)
        for i in range(BLOCK // 128):
            at = (b * (BLOCK // 128) + i) * head_dim
            sent_state[at : at + head_dim, :] = own[:, i * 128 : (i + 1) * 128]
    key_sum = jnp.sum(sum_acc[...], axis=0, keepdims=True)
    high = key_sum.astype(BF16).astype(F32)
    line = lax.broadcasted_iota(jnp.int32, (16, 128), 0)
    packed = jnp.zeros((16, 128), F32)
    for i in range(pieces):
        lanes = slice(i * 128, (i + 1) * 128)
        packed = jnp.where(line == i, high[:, lanes], packed)
        packed = jnp.where(line == pieces + i, (key_sum - high)[:, lanes], packed)
    sent_state[sum_at : sum_at + 16, :] = packed.astype(BF16)

    all_state[me] = sent_state[...]

    pl.semaphore_wait(barrier, n - 1)

    @pl.loop(1, levels)
    def _(k):
        column_copy(k).start()

    row_pass(0).start()
    core_pass(0, 0).start()

    permute(targets[0])
    send_tiles(targets[0])
    permute(targets[1])
    send_tiles(targets[1])

    @pl.loop(0, chunks // 2)
    def _(k):
        permute(facing((1 - k) * (2 - inward) + k * 3))

    tile_tokens[mine] = sent_tokens[mine]

    send_tiles(targets[2])
    send_tiles(targets[3])

    @pl.loop(1, levels)
    def _(k):
        column_copy(k).wait_recv()
        row_pass(k).start()
        core_pass(k, 0).start()

    @pl.loop(0, levels)
    def _(k):
        row_pass(k).wait_recv()
        core_pass(k, 1).start()

    def attend_order(k):
        if k < 2:
            return facing(inward + k * (1 - 2 * inward))
        return facing((3 - k) * (3 - inward) + (k - 2) * (2 + inward))

    def queries(c):
        @pl.loop(0, share)
        def _(k):
            source = c * share + k

            @pl.when(source != mine)
            def _():
                tok_arrival(source).wait_recv()

        mixed = jnp.dot(
            flat(tile_tokens[pl.ds(c * share, share)]),
            qkv_ref[:, 0:width],
            preferred_element_type=F32,
        ).astype(BF16)
        rows = pl.ds(pl.multiple_of(c * CHUNK, CHUNK), CHUNK)
        rows_ref[rows, :] = jnp.maximum(mixed, jnp.zeros((), BF16)).astype(F32)

    for k in range(2):
        queries(attend_order(k))

    @pl.loop(0, levels)
    def _(k):
        core_pass(k, 0).wait_recv()
        core_pass(k, 1).wait_recv()

    running[...] = jnp.zeros_like(running)
    prefix[...] = jnp.zeros_like(prefix)

    @pl.loop(0, n)
    def _(f):
        new_group = group_ref[f] != group_ref[jnp.maximum(f - 1, 0)]
        before = jnp.where(new_group, running[...], prefix[...])
        prefix[...] = before
        own = all_state[f].astype(F32)
        running[...] += own
        all_total[f] = before + own

    head_ones = same_head.astype(F32).astype(BF16)
    reach = 3 * channels

    def attend_chunk(c):
        rows = pl.ds(pl.multiple_of(c * CHUNK, CHUNK), CHUNK)

        def attend(k, carry):
            total = all_total[frame_of(c * share + k, y)]
            key_total = jnp.concatenate(
                [
                    total[sum_at + i : sum_at + i + 1, :]
                    + total[sum_at + pieces + i : sum_at + pieces + i + 1, :]
                    for i in range(pieces)
                ],
                axis=1,
            )
            here = pl.ds(pl.multiple_of(c * CHUNK + k * pair_tokens, 16), pair_tokens)
            query = rows_ref[here, :]
            scaled = (query * key_total).astype(BF16)
            query = query.astype(BF16)
            for b in range(blocks):
                lanes = slice(b * BLOCK, (b + 1) * BLOCK)
                first = b * (BLOCK // 128)
                state = jnp.concatenate(
                    [
                        total[i * head_dim : (i + 1) * head_dim, :]
                        for i in range(first, first + BLOCK // 128)
                    ],
                    axis=1,
                )
                high = state.astype(BF16).astype(F32)
                numer = jnp.zeros((pair_tokens, BLOCK), F32)
                for part in (high, state - high):
                    spread = jnp.concatenate([part] * heads_per, axis=0)
                    spread = jnp.where(same_head, spread, 0.0).astype(BF16)
                    numer += jnp.dot(query[:, lanes], spread, preferred_element_type=F32)
                denom = jnp.dot(scaled[:, lanes], head_ones, preferred_element_type=F32) + 1.0
                rows_ref[here, lanes] = numer / denom
            return carry

        lax.fori_loop(0, share, attend, 0, unroll=share <= 4)
        attended = rows_ref[rows, :].reshape(share, 2, row_tokens, width)
        for i in range(2):
            made[i, c] = attended[:, i].astype(BF16)
        made_copy(0, c).start()
        made_copy(2, c).start()

        @pl.when(across == 0)
        def _():
            made_copy(3, c).start()

        @pl.when(exists)
        def _():
            made_copy(1, c).start()

        @pl.when(across == 0)
        def _():
            near_rows[1, c, y] = made[core, c]
            near_rows[peer_slot, c, y] = made[1 - core, c]

        @pl.when(across == 1)
        def _():
            near_rows[far_slot, c, y] = made[1 - core, c]

    for k in range(2):
        attend_chunk(attend_order(k))

    loads[2].wait()
    loads[3].wait()

    def widen(even, odd):
        column = lax.rem(lax.broadcasted_iota(jnp.int32, even.shape, 0), row_tokens)
        odd_left = jnp.where(column == 0, 0.0, pltpu.roll(odd, 1, 0))
        even_right = jnp.where(column == row_tokens - 1, 0.0, pltpu.roll(even, CHUNK - 1, 0))
        return [x.astype(BF16) for x in (odd_left, even, odd, even_right)]

    valid = valid_ref[me]
    valid_above = jnp.where(me > 0, valid_ref[jnp.maximum(me - 1, 0)], 0)
    valid_below = jnp.where(me < n - 1, valid_ref[jnp.minimum(me + 1, n - 1)], 0)
    valid_rows = valid * row_tokens

    outer = across == 0
    half = 2 * channels
    limits = (valid_above, valid, valid, valid_below)

    def frames_here():
        row = lax.broadcasted_iota(jnp.int32, (CHUNK, channels), 0)
        step = lax.div(row, row_tokens)
        return lax.rem(step, share), lax.div(step, share)

    def chunk_frames(c):
        k, column = frames_here()
        return frame_of(c * share + k, column)

    def place_line(p, line, frame, limit):
        live = frame < limit
        even = jnp.where(live, line[:, :channels], 0.0)
        odd = jnp.where(live, line[:, channels:], 0.0)
        for i, part in enumerate(widen(even, odd)):
            cells[p, :, i * channels : (i + 1) * channels] = part

    def out_pixels(c, b):
        return pl.ds(c * 2 * CHUNK + b, CHUNK, 2)

    def gather_stats(c, r, results, live):
        eights = [x.reshape(CHUNK // 8, 8, channels).sum(axis=0) for x in results]
        total = jnp.sum(eights[0] + eights[1], axis=0, keepdims=True)
        size = jnp.clip(valid_rows - c * CHUNK, 0, CHUNK) * 2
        centre = total / jnp.maximum(size, 1).astype(F32)
        square = jnp.zeros((8, channels), F32)
        for x in results:
            off = jnp.where(live, x - centre, 0.0)
            square += (off * off).reshape(CHUNK // 8, 8, channels).sum(axis=0)
        square = jnp.sum(square, axis=0, keepdims=True)
        line = lax.broadcasted_iota(jnp.int32, (8, channels), 0)
        stat_acc[2 * c + r] = jnp.where(
            line == 0, total, jnp.where(line == 1, square, size.astype(F32))
        )

    def decode(c, defer):
        near_arrival(1, c, 1 - y).wait_recv()
        relay_copy(c).start()

        @pl.when(jnp.logical_not(outer))
        def _():
            near_arrival(1, c, y).wait_recv()
            near_arrival(peer_slot, c, y).wait_recv()
            near_arrival(far_slot, c, 1 - y).wait_recv()

        if not defer:

            @pl.when(jnp.logical_and(outer, exists))
            def _():
                near_arrival(far_slot, c, y).wait_recv()
                near_arrival(far_slot, c, 1 - y).wait_recv()

        frame = chunk_frames(c)
        own = jnp.dot(flat(near_rows[1, c]), outw_ref[...], preferred_element_type=F32)
        place_line(1, own[:, :half], frame, valid)
        place_line(2, own[:, half:], frame, valid)
        near_arrival(peer_slot, c, 1 - y).wait_recv()
        absent = outer if defer else jnp.logical_and(outer, jnp.logical_not(exists))
        for p, slot, low in ((0, 0, half), (3, 2, 0)):
            missing = jnp.logical_and(absent, far_slot == slot)

            @pl.when(missing)
            def _():
                cells[p] = jnp.zeros(cells.shape[1:], BF16)

            @pl.when(jnp.logical_not(missing))
            def _():
                line = jnp.dot(
                    flat(near_rows[slot, c]),
                    outw_ref[:, low : low + half],
                    preferred_element_type=F32,
                )
                place_line(p, line, frame, limits[p])

        live = frame < valid
        for r in range(2):
            results = []
            for b in range(2):
                lanes = slice(b * channels, b * channels + reach)
                result = sum(
                    jnp.dot(cells[r + d, :, lanes], convw_ref[d], preferred_element_type=F32)
                    for d in range(3)
                )
                result = jnp.where(live, result, 0.0)
                results.append(result)
                for h in range(0, channels, 128):
                    out_buf[r, h // 128, out_pixels(c, b), :] = result[:, h : h + 128]
            gather_stats(c, r, results, live)

    def finish(c):
        near_arrival(far_slot, c, y).wait_recv()
        near_arrival(far_slot, c, 1 - y).wait_recv()
        frame = chunk_frames(c)
        line = jnp.dot(
            flat(near_rows[far_slot, c]),
            outw_ref[:, pl.ds(pl.multiple_of((1 - core) * half, half), half)],
            preferred_element_type=F32,
        )
        place_line(0, line, frame, jnp.where(core == 0, valid_above, valid_below))
        live = frame < valid
        results = []
        for b in range(2):
            lanes = slice(b * channels, b * channels + reach)
            result = jnp.dot(cells[0, :, lanes], convw_ref[far_slot], preferred_element_type=F32)
            before = jnp.concatenate(
                [out_buf[core, h, out_pixels(c, b), :] for h in range(channels // 128)], axis=1
            )
            result = before + jnp.where(live, result, 0.0)
            results.append(result)
            for h in range(0, channels, 128):
                out_buf[core, h // 128, out_pixels(c, b), :] = result[:, h : h + 128]
        gather_stats(c, core, results, live)

    for k in range(2, 4):
        queries(attend_order(k))
        attend_chunk(attend_order(k))

    def decode_order(k):
        return facing(k + lax.div(k, 2))

    @pl.loop(0, 3)
    def _(k):
        decode(decode_order(k), True)

    @pl.when(jnp.logical_and(outer, exists))
    def _():
        @pl.loop(0, 3)
        def _(k):
            finish(decode_order(k))

    decode(facing(2), False)

    group_row = lax.broadcasted_iota(jnp.int32, (channels, channels), 0) // group_size
    group_col = lax.broadcasted_iota(jnp.int32, (channels, channels), 1) // group_size
    group_ones = jnp.where(group_row == group_col, 1.0, 0.0).astype(BF16)

    def group_total(sums):
        parts = []
        for _ in range(3):
            part = sums.astype(BF16)
            parts.append(part)
            sums = sums - part.astype(F32)
        line = lax.broadcasted_iota(jnp.int32, (16, channels), 0)
        stacked = jnp.zeros((16, channels), F32)
        for i, part in enumerate(parts):
            stacked = jnp.where(line == i, part.astype(F32), stacked)
        found = jnp.dot(stacked.astype(BF16), group_ones, preferred_element_type=F32)
        return found[0:1] + found[1:2] + found[2:3]

    def combine(field):
        total, square, size = [field[:, i, :] for i in range(3)]
        whole = jnp.sum(size, axis=0, keepdims=True)
        mean = jnp.sum(total, axis=0, keepdims=True) / whole
        off = total / jnp.maximum(size, 1.0) - mean
        return mean, jnp.sum(square + size * (off * off), axis=0, keepdims=True), whole

    mean, square, whole = combine(stat_acc)
    line = lax.broadcasted_iota(jnp.int32, (8, channels), 0)
    sent_stat[...] = jnp.where(line == 0, mean * whole, jnp.where(line == 1, square, whole))

    @pl.loop(1, n)
    def _(s):
        stat_copy(s).start()

    all_stat[me] = sent_stat[...]

    @pl.loop(1, n)
    def _(s):
        stat_copy(s).wait_recv()

    mean, square, whole = combine(all_stat)
    group_mean = group_total(mean) / group_size
    off = mean - group_mean
    group_square = group_total(square + whole * (off * off))
    mean = group_mean
    scale = gain_ref[...] * lax.rsqrt(group_square / (whole * group_size) + 1e-05)
    sides = [(r, h) for r in range(2) for h in range(channels // 128)]
    half_scale = 0.5 * scale
    half_shift = 0.5 * (bias_ref[...] - mean * scale)

    @pl.loop(0, n)
    def _(s):
        pixels = pl.ds(pl.multiple_of(s * 2 * row_tokens, 8), 2 * row_tokens)
        step = lax.rem(s, 2 * share)
        f = frame_of(lax.div(s, 2 * share) * share + lax.rem(step, share), lax.div(step, share))
        live = f < valid
        for r, h in sides:
            lanes = slice(h * 128, (h + 1) * 128)
            normed = out_buf[r, h, pixels, :] * half_scale[:, lanes] + half_shift[:, lanes]
            silu = normed + normed * jnp.tanh(normed)
            decoded_ref[f, r, :, lanes] = jnp.where(live, silu, 0.0).astype(BF16)

    @pl.loop(0, n // 2)
    def _(slot):
        @pl.when(slot != mine)
        def _():
            tok_copy(slot).wait_send()

    @pl.loop(0, chunks)
    def _(c):
        made_copy(0, c).wait_send()
        made_copy(2, c).wait_send()
        relay_copy(c).wait_send()

        @pl.when(across == 0)
        def _():
            made_copy(3, c).wait_send()

        @pl.when(exists)
        def _():
            made_copy(1, c).wait_send()

    @pl.loop(1, n)
    def _(s):
        stat_copy(s).wait_send()

    @pl.loop(1, levels)
    def _(k):
        column_copy(k).wait_send()

    @pl.loop(0, levels)
    def _(k):
        row_pass(k).wait_send()
        core_pass(k, 0).wait_send()
        core_pass(k, 1).wait_send()


def local(
    tokens,
    qkv_weight,
    out_weight,
    conv_weight,
    norm_gain,
    norm_bias,
    group_map,
    token_order,
    valid_frames,
):
    n = lax.axis_size("tm")
    count, width = tokens.shape
    channels = conv_weight.shape[3]
    row_tokens = count // n
    chunks = count // CHUNK
    share = n // (2 * chunks)
    state_shape = (width // 128 * (width // HEADS) + 16, 128)
    anywhere = pl.BlockSpec(memory_space=pltpu.HBM)
    vmem = pl.BlockSpec(memory_space=pltpu.VMEM)
    smem = pl.BlockSpec(memory_space=pltpu.SMEM)
    dma = pltpu.SemaphoreType.DMA
    return pl.pallas_call(
        functools.partial(mega, n),
        out_shape=pltpu.VMEM((n, 2, 2 * row_tokens, channels), BF16),
        in_specs=[anywhere] * 4 + [vmem, vmem, smem, vmem, smem],
        out_specs=vmem,
        scratch_shapes=[
            pltpu.VMEM((count, width), BF16),
            pltpu.VMEM((width, 3 * width), BF16),
            pltpu.VMEM((width, 4 * channels), BF16),
            pltpu.VMEM((3, 3 * channels, channels), BF16),
            pltpu.VMEM((n // 2, 2 * row_tokens, width), BF16),
            pltpu.VMEM((n // 2, 2 * row_tokens, width), BF16),
            pltpu.VMEM((width // BLOCK, BLOCK, BLOCK), F32),
            pltpu.VMEM((8, width), F32),
            pltpu.VMEM(state_shape, BF16),
            pltpu.VMEM((n,) + state_shape, BF16),
            pltpu.VMEM((n,) + state_shape, F32),
            pltpu.VMEM(state_shape, F32),
            pltpu.VMEM(state_shape, F32),
            pltpu.VMEM((count, width), F32),
            pltpu.VMEM((2, chunks, share, row_tokens, width), BF16),
            pltpu.VMEM((3, chunks, 2, share, row_tokens, width), BF16),
            pltpu.VMEM((4, CHUNK, 4 * channels), BF16),
            pltpu.VMEM((2 * chunks, 8, channels), F32),
            pltpu.VMEM((8, channels), F32),
            pltpu.VMEM((n, 8, channels), F32),
            pltpu.VMEM((2, channels // 128, 2 * count, 128), F32),
            dma((4,)),
            dma((n // 2,)),
            dma((n // 2,)),
            dma((2, n // 4)),
            dma((2, n // 4)),
            dma((n // 4,)),
            dma((n // 4,)),
            dma((n // 4,)),
            dma((n // 4,)),
            dma((4, chunks)),
            dma((chunks,)),
            dma((3, chunks, 2)),
            dma((n,)),
            dma((n,)),
        ],
        compiler_params=pltpu.CompilerParams(
            collective_id=0, has_side_effects=True, vmem_limit_bytes=VMEM - 2 * count * 4 * channels
        ),
    )(
        tokens,
        qkv_weight,
        out_weight,
        conv_weight.reshape(3, 3 * channels, channels),
        norm_gain[None],
        norm_bias[None],
        group_map,
        token_order[None],
        valid_frames,
    )


def solution(mesh):
    in_specs = (P(("clip", "tm"), None), P(), P(), P(), P(), P(), P("clip"), P("clip"), P("clip"))
    out_specs = P("clip", "tm", None, None)
    return jax.shard_map(local, mesh=mesh, in_specs=in_specs, out_specs=out_specs, check_vma=False)
```

```python
import functools

import jax
import jax.numpy as jnp
from jax import lax
from jax.experimental import pallas as pl
from jax.experimental.pallas import tpu as pltpu
from jax.sharding import PartitionSpec as P

HEADS = 16
NORM_GROUPS = 32
MESH = pl.DeviceIdType.MESH
F32 = jnp.float32
BF16 = jnp.bfloat16
CHUNK = 256
BLOCK = 256
VMEM = 66650112


def flat(cells):
    rows, width = cells.shape[-2:]
    every = cells.size // width
    if rows % 16 == 0:
        return cells.reshape(every, width)
    return cells.astype(F32).reshape(every, width).astype(BF16)


def mega(
    n,
    tokens_hbm,
    qkv_hbm,
    out_hbm,
    conv_hbm,
    gain_ref,
    bias_ref,
    group_ref,
    order_ref,
    valid_ref,
    decoded_ref,
    tokens_ref,
    qkv_ref,
    outw_ref,
    convw_ref,
    sent_tokens,
    tile_tokens,
    state_acc,
    sum_acc,
    sent_state,
    all_state,
    all_total,
    running,
    prefix,
    rows_ref,
    made,
    near_rows,
    cells,
    stat_acc,
    sent_stat,
    all_stat,
    out_buf,
    load_sem,
    tok_send,
    tok_recv,
    core_send,
    core_recv,
    col_send,
    col_recv,
    row_send,
    row_recv,
    made_send,
    relay_send,
    near_recv,
    stat_send,
    stat_recv,
):
    me = lax.axis_index("tm")
    count, width = tokens_ref.shape
    row_tokens = count // n
    pair_tokens = 2 * row_tokens
    chunks = count // CHUNK
    share = n // (2 * chunks)
    head_dim = width // HEADS
    channels = gain_ref.shape[1]
    blocks = width // BLOCK
    heads_per = BLOCK // head_dim
    group_size = channels // NORM_GROUPS

    levels = n // 4
    level = lax.div(me, 4)
    y = lax.rem(lax.div(me, 2), 2)
    core = lax.rem(me, 2)
    side = lax.div(me, n // 2)
    place = lax.div(me, n // chunks)
    inward = place + side * (chunks - 1 - 2 * place)
    inner = inward == 1
    mine = 2 * level + core
    core_peer = me + 1 - 2 * core
    row_peer = me + 2 - 4 * y

    def facing(k):
        return k + side * (chunks - 1 - 2 * k)

    def frame_of(source, column):
        return 4 * lax.div(source, 2) + 2 * column + lax.rem(source, 2)

    loads = [
        pltpu.make_async_copy(a, b, load_sem.at[i])
        for i, (a, b) in enumerate(
            [
                (tokens_hbm, tokens_ref),
                (qkv_hbm, qkv_ref),
                (out_hbm, outw_ref),
                (conv_hbm, convw_ref),
            ]
        )
    ]
    for load in loads:
        load.start()

    barrier = pltpu.get_barrier_semaphore()

    @pl.loop(1, n)
    def _(s):
        pl.semaphore_signal(
            barrier, inc=1, device_id={"tm": lax.rem(me + s, n)}, device_id_type=MESH
        )

    def remote(src, dst, send_sem, recv_sem, device):
        return pltpu.make_async_remote_copy(
            src_ref=src,
            dst_ref=dst,
            send_sem=send_sem,
            recv_sem=recv_sem,
            device_id={"tm": device},
            device_id_type=MESH,
        )

    def tok_copy(slot):
        return remote(
            sent_tokens.at[slot],
            tile_tokens.at[mine],
            tok_send.at[slot],
            tok_recv.at[mine],
            4 * lax.div(slot, 2) + 2 * y + lax.rem(slot, 2),
        )

    def tok_arrival(source):
        return remote(
            sent_tokens.at[source],
            tile_tokens.at[source],
            tok_send.at[source],
            tok_recv.at[source],
            4 * lax.div(source, 2) + 2 * y + lax.rem(source, 2),
        )

    def column_copy(k):
        return remote(
            sent_state,
            all_state.at[me],
            col_send.at[k],
            col_recv.at[k],
            lax.rem(me + 4 * k, n),
        )

    def pass_on(source, peer, send_sem, recv_sem):
        return remote(all_state.at[source], all_state.at[source], send_sem, recv_sem, peer)

    def row_pass(k):
        source = lax.rem(me + n - 4 * k, n)
        return pass_on(source, row_peer, row_send.at[k], row_recv.at[k])

    def core_pass(k, d):
        source = lax.rem(me + d * (row_peer - me) + n - 4 * k, n)
        return pass_on(source, core_peer, core_send.at[d, k], core_recv.at[d, k])

    def stat_copy(s):
        return remote(
            sent_stat,
            all_stat.at[me],
            stat_send.at[s],
            stat_recv.at[s],
            lax.rem(me + s, n),
        )

    across = lax.rem(y + core, 2)
    outer_owner = 4 * level + 3 * core
    inner_owner = 4 * level + 1 + core
    beyond = 4 * level - 1 + 5 * core
    exists = jnp.logical_and(beyond >= 0, beyond < n)
    beyond_device = jnp.clip(beyond, 0, n - 1)
    far_slot = 2 * core
    peer_slot = 2 - 2 * core

    def made_copy(kind, c):
        if kind == 0:
            part, device, slot = 1 - core, inner_owner, 1
        elif kind == 1:
            part, device, slot = core, beyond_device, peer_slot
        elif kind == 2:
            part = core
            device = across * outer_owner + (1 - across) * inner_owner
            slot = across + (1 - across) * far_slot
        else:
            part, device, slot = 1 - core, 4 * level + 2 - core, far_slot
        return remote(
            made.at[part, c],
            near_rows.at[slot, c, y],
            made_send.at[kind, c],
            near_recv.at[slot, c, y],
            device,
        )

    def relay_copy(c):
        return remote(
            near_rows.at[1, c, 1 - y],
            near_rows.at[far_slot, c, 1 - y],
            relay_send.at[c],
            near_recv.at[far_slot, c, 1 - y],
            core_peer,
        )

    def near_arrival(slot, c, column):
        return remote(
            near_rows.at[slot, c, column],
            near_rows.at[slot, c, column],
            made_send.at[0, c],
            near_recv.at[slot, c, column],
            core_peer,
        )

    loads[0].wait()

    def permute(to):
        where = lax.broadcasted_iota(jnp.int32, (CHUNK, count), 0) + to * CHUNK
        pick = jnp.where(order_ref[...] == where, 1.0, 0.0).astype(BF16)
        moved = jnp.dot(pick, tokens_ref[...], preferred_element_type=F32)
        sent_tokens[pl.ds(to * share, share)] = moved.reshape(share, pair_tokens, width).astype(
            BF16
        )

    def send_tiles(to):
        @pl.loop(0, share)
        def _(k):
            slot = to * share + k

            @pl.when(slot != mine)
            def _():
                tok_copy(slot).start()

    targets = [facing(x) for x in (inward + 1, inward * 0, 2 - inward, inward * 0 + 3)]

    loads[1].wait()
    state_acc[...] = jnp.zeros_like(state_acc)
    sum_acc[...] = jnp.zeros_like(sum_acc)

    @pl.loop(0, chunks)
    def _(c):
        rows = pl.ds(pl.multiple_of(c * CHUNK, CHUNK), CHUNK)
        mixed = jnp.dot(
            tokens_ref[rows, :], qkv_ref[:, width : 3 * width], preferred_element_type=F32
        ).astype(BF16)
        keys = jnp.maximum(mixed[:, :width], jnp.zeros((), BF16))
        sum_acc[...] += keys.astype(F32).reshape(CHUNK // 8, 8, width).sum(axis=0)
        for b in range(blocks):
            lanes = slice(b * BLOCK, (b + 1) * BLOCK)
            state_acc[b] += lax.dot_general(
                keys[:, lanes],
                mixed[:, width + b * BLOCK : width + (b + 1) * BLOCK],
                (((0,), (0,)), ((), ())),
                preferred_element_type=F32,
            )

    head_row = lax.broadcasted_iota(jnp.int32, (BLOCK, BLOCK), 0) // head_dim
    head_col = lax.broadcasted_iota(jnp.int32, (BLOCK, BLOCK), 1) // head_dim
    same_head = head_row == head_col
    pieces = width // 128
    sum_at = pieces * head_dim
    for b in range(blocks):
        own = jnp.where(same_head, state_acc[b], 0.0)
        own = own.reshape(heads_per, head_dim, BLOCK).sum(axis=0).astype(BF16)
        for i in range(BLOCK // 128):
            at = (b * (BLOCK // 128) + i) * head_dim
            sent_state[at : at + head_dim, :] = own[:, i * 128 : (i + 1) * 128]
    key_sum = jnp.sum(sum_acc[...], axis=0, keepdims=True)
    high = key_sum.astype(BF16).astype(F32)
    line = lax.broadcasted_iota(jnp.int32, (16, 128), 0)
    packed = jnp.zeros((16, 128), F32)
    for i in range(pieces):
        lanes = slice(i * 128, (i + 1) * 128)
        packed = jnp.where(line == i, high[:, lanes], packed)
        packed = jnp.where(line == pieces + i, (key_sum - high)[:, lanes], packed)
    sent_state[sum_at : sum_at + 16, :] = packed.astype(BF16)

    all_state[me] = sent_state[...]

    pl.semaphore_wait(barrier, n - 1)

    @pl.loop(1, levels)
    def _(k):
        column_copy(k).start()

    row_pass(0).start()
    core_pass(0, 0).start()

    permute(targets[0])
    send_tiles(targets[0])
    permute(targets[1])
    send_tiles(targets[1])

    @pl.loop(0, chunks // 2)
    def _(k):
        permute(facing((1 - k) * (2 - inward) + k * 3))

    tile_tokens[mine] = sent_tokens[mine]

    send_tiles(targets[2])
    send_tiles(targets[3])

    @pl.loop(1, levels)
    def _(k):
        column_copy(k).wait_recv()
        row_pass(k).start()
        core_pass(k, 0).start()

    @pl.loop(0, levels)
    def _(k):
        row_pass(k).wait_recv()
        core_pass(k, 1).start()

    def attend_order(k):
        late = lax.div(k, 2)
        return facing(
            (1 - late) * (inward + k * (1 - 2 * inward))
            + late * ((3 - k) * (3 - inward) + (k - 2) * (2 + inward))
        )

    def queries(c):
        @pl.loop(0, share)
        def _(k):
            source = c * share + k

            @pl.when(source != mine)
            def _():
                tok_arrival(source).wait_recv()

        mixed = jnp.dot(
            flat(tile_tokens[pl.ds(c * share, share)]),
            qkv_ref[:, 0:width],
            preferred_element_type=F32,
        ).astype(BF16)
        rows = pl.ds(pl.multiple_of(c * CHUNK, CHUNK), CHUNK)
        rows_ref[rows, :] = jnp.maximum(mixed, jnp.zeros((), BF16)).astype(F32)

    for k in range(2):
        queries(attend_order(k))

    @pl.loop(0, levels)
    def _(k):
        core_pass(k, 0).wait_recv()
        core_pass(k, 1).wait_recv()

    running[...] = jnp.zeros_like(running)
    prefix[...] = jnp.zeros_like(prefix)

    @pl.loop(0, n)
    def _(f):
        new_group = group_ref[f] != group_ref[jnp.maximum(f - 1, 0)]
        before = jnp.where(new_group, running[...], prefix[...])
        prefix[...] = before
        own = all_state[f].astype(F32)
        running[...] += own
        all_total[f] = before + own

    head_ones = same_head.astype(F32).astype(BF16)
    reach = 3 * channels

    def attend_chunk(c):
        rows = pl.ds(pl.multiple_of(c * CHUNK, CHUNK), CHUNK)

        def attend(k, carry):
            total = all_total[frame_of(c * share + k, y)]
            key_total = jnp.concatenate(
                [
                    total[sum_at + i : sum_at + i + 1, :]
                    + total[sum_at + pieces + i : sum_at + pieces + i + 1, :]
                    for i in range(pieces)
                ],
                axis=1,
            )
            here = pl.ds(pl.multiple_of(c * CHUNK + k * pair_tokens, 16), pair_tokens)
            query = rows_ref[here, :]
            scaled = (query * key_total).astype(BF16)
            query = query.astype(BF16)
            for b in range(blocks):
                lanes = slice(b * BLOCK, (b + 1) * BLOCK)
                first = b * (BLOCK // 128)
                state = jnp.concatenate(
                    [
                        total[i * head_dim : (i + 1) * head_dim, :]
                        for i in range(first, first + BLOCK // 128)
                    ],
                    axis=1,
                )
                high = state.astype(BF16).astype(F32)
                numer = jnp.zeros((pair_tokens, BLOCK), F32)
                for part in (high, state - high):
                    spread = jnp.concatenate([part] * heads_per, axis=0)
                    spread = jnp.where(same_head, spread, 0.0).astype(BF16)
                    numer += jnp.dot(query[:, lanes], spread, preferred_element_type=F32)
                denom = jnp.dot(scaled[:, lanes], head_ones, preferred_element_type=F32) + 1.0
                rows_ref[here, lanes] = numer / denom
            return carry

        lax.fori_loop(0, share, attend, 0, unroll=share <= 4)
        attended = rows_ref[rows, :].reshape(share, 2, row_tokens, width)
        for i in range(2):
            made[i, c] = attended[:, i].astype(BF16)
        made_copy(0, c).start()
        made_copy(2, c).start()

        @pl.when(across == 0)
        def _():
            made_copy(3, c).start()

        @pl.when(across == 0)
        def _():
            near_rows[1, c, y] = made[core, c]
            near_rows[peer_slot, c, y] = made[1 - core, c]

        @pl.when(across == 1)
        def _():
            near_rows[far_slot, c, y] = made[1 - core, c]

    for k in range(2):
        attend_chunk(attend_order(k))

    loads[2].wait()
    loads[3].wait()

    def widen(even, odd):
        column = lax.rem(lax.broadcasted_iota(jnp.int32, even.shape, 0), row_tokens)
        odd_left = jnp.where(column == 0, 0.0, pltpu.roll(odd, 1, 0))
        even_right = jnp.where(column == row_tokens - 1, 0.0, pltpu.roll(even, CHUNK - 1, 0))
        return [x.astype(BF16) for x in (odd_left, even, odd, even_right)]

    valid = valid_ref[me]
    valid_above = jnp.where(me > 0, valid_ref[jnp.maximum(me - 1, 0)], 0)
    valid_below = jnp.where(me < n - 1, valid_ref[jnp.minimum(me + 1, n - 1)], 0)
    valid_rows = valid * row_tokens

    outer = across == 0
    half = 2 * channels
    limits = (valid_above, valid, valid, valid_below)

    def frames_here():
        row = lax.broadcasted_iota(jnp.int32, (CHUNK, channels), 0)
        step = lax.div(row, row_tokens)
        return lax.rem(step, share), lax.div(step, share)

    def chunk_frames(c):
        k, column = frames_here()
        return frame_of(c * share + k, column)

    def place_line(p, line, frame, limit):
        live = frame < limit
        even = jnp.where(live, line[:, :channels], 0.0)
        odd = jnp.where(live, line[:, channels:], 0.0)
        for i, part in enumerate(widen(even, odd)):
            cells[p, :, i * channels : (i + 1) * channels] = part

    def out_pixels(c, b):
        return pl.ds(c * 2 * CHUNK + b, CHUNK, 2)

    def gather_stats(c, r, results, live):
        eights = [x.reshape(CHUNK // 8, 8, channels).sum(axis=0) for x in results]
        total = jnp.sum(eights[0] + eights[1], axis=0, keepdims=True)
        size = jnp.clip(valid_rows - c * CHUNK, 0, CHUNK) * 2
        centre = total / jnp.maximum(size, 1).astype(F32)
        square = jnp.zeros((8, channels), F32)
        for x in results:
            off = jnp.where(live, x - centre, 0.0)
            square += (off * off).reshape(CHUNK // 8, 8, channels).sum(axis=0)
        square = jnp.sum(square, axis=0, keepdims=True)
        line = lax.broadcasted_iota(jnp.int32, (8, channels), 0)
        stat_acc[2 * c + r] = jnp.where(
            line == 0, total, jnp.where(line == 1, square, size.astype(F32))
        )

    def relay(c):
        near_arrival(1, c, 1 - y).wait_recv()
        relay_copy(c).start()

    def decode(c, defer):
        @pl.when(jnp.logical_not(outer))
        def _():
            near_arrival(1, c, y).wait_recv()
            near_arrival(peer_slot, c, y).wait_recv()
            near_arrival(far_slot, c, 1 - y).wait_recv()

        if not defer:

            @pl.when(jnp.logical_and(outer, exists))
            def _():
                near_arrival(far_slot, c, y).wait_recv()
                near_arrival(far_slot, c, 1 - y).wait_recv()

        frame = chunk_frames(c)
        own = jnp.dot(flat(near_rows[1, c]), outw_ref[...], preferred_element_type=F32)
        place_line(1, own[:, :half], frame, valid)
        place_line(2, own[:, half:], frame, valid)
        near_arrival(peer_slot, c, 1 - y).wait_recv()
        absent = outer if defer else jnp.logical_and(outer, jnp.logical_not(exists))
        for p, slot, low in ((0, 0, half), (3, 2, 0)):
            missing = jnp.logical_and(absent, far_slot == slot)

            @pl.when(missing)
            def _():
                cells[p] = jnp.zeros(cells.shape[1:], BF16)

            @pl.when(jnp.logical_not(missing))
            def _():
                line = jnp.dot(
                    flat(near_rows[slot, c]),
                    outw_ref[:, low : low + half],
                    preferred_element_type=F32,
                )
                place_line(p, line, frame, limits[p])

        live = frame < valid
        for r in range(2):
            results = []
            for b in range(2):
                lanes = slice(b * channels, b * channels + reach)
                result = sum(
                    jnp.dot(cells[r + d, :, lanes], convw_ref[d], preferred_element_type=F32)
                    for d in range(3)
                )
                result = jnp.where(live, result, 0.0)
                results.append(result)
                for h in range(0, channels, 128):
                    out_buf[r, h // 128, out_pixels(c, b), :] = result[:, h : h + 128]
            gather_stats(c, r, results, live)

    def finish(c):
        near_arrival(far_slot, c, y).wait_recv()
        near_arrival(far_slot, c, 1 - y).wait_recv()
        frame = chunk_frames(c)
        line = jnp.dot(
            flat(near_rows[far_slot, c]),
            outw_ref[:, pl.ds(pl.multiple_of((1 - core) * half, half), half)],
            preferred_element_type=F32,
        )
        place_line(0, line, frame, jnp.where(core == 0, valid_above, valid_below))
        live = frame < valid
        results = []
        for b in range(2):
            lanes = slice(b * channels, b * channels + reach)
            result = jnp.dot(cells[0, :, lanes], convw_ref[far_slot], preferred_element_type=F32)
            before = jnp.concatenate(
                [out_buf[core, h, out_pixels(c, b), :] for h in range(channels // 128)], axis=1
            )
            result = before + jnp.where(live, result, 0.0)
            results.append(result)
            for h in range(0, channels, 128):
                out_buf[core, h // 128, out_pixels(c, b), :] = result[:, h : h + 128]
        gather_stats(c, core, results, live)

    def reach_beyond(*steps):
        @pl.when(exists)
        def _():
            for k in steps:
                made_copy(1, attend_order(k)).start()

    def first_decode():
        decode(attend_order(0), True)

    @pl.when(jnp.logical_and(inner, core == 1))
    def _():
        relay(attend_order(0))
        first_decode()

    @pl.when(jnp.logical_not(inner))
    def _():
        relay(attend_order(0))

    queries(attend_order(2))
    attend_chunk(attend_order(2))
    reach_beyond(0, 1)

    @pl.when(jnp.logical_not(inner))
    def _():
        first_decode()

    queries(attend_order(3))
    attend_chunk(attend_order(3))
    reach_beyond(2, 3)

    @pl.when(jnp.logical_and(inner, core == 0))
    def _():
        relay(attend_order(0))
        first_decode()

    relay(attend_order(1))

    decode(attend_order(1), True)
    relay(attend_order(2))
    decode(attend_order(2), True)

    @pl.when(jnp.logical_and(outer, exists))
    def _():
        @pl.loop(0, 3)
        def _(k):
            finish(attend_order(k))

    relay(attend_order(3))
    decode(attend_order(3), False)

    group_row = lax.broadcasted_iota(jnp.int32, (channels, channels), 0) // group_size
    group_col = lax.broadcasted_iota(jnp.int32, (channels, channels), 1) // group_size
    group_ones = jnp.where(group_row == group_col, 1.0, 0.0).astype(BF16)

    def group_total(sums):
        parts = []
        for _ in range(3):
            part = sums.astype(BF16)
            parts.append(part)
            sums = sums - part.astype(F32)
        line = lax.broadcasted_iota(jnp.int32, (16, channels), 0)
        stacked = jnp.zeros((16, channels), F32)
        for i, part in enumerate(parts):
            stacked = jnp.where(line == i, part.astype(F32), stacked)
        found = jnp.dot(stacked.astype(BF16), group_ones, preferred_element_type=F32)
        return found[0:1] + found[1:2] + found[2:3]

    def combine(field):
        total, square, size = [field[:, i, :] for i in range(3)]
        whole = jnp.sum(size, axis=0, keepdims=True)
        mean = jnp.sum(total, axis=0, keepdims=True) / whole
        off = total / jnp.maximum(size, 1.0) - mean
        return mean, jnp.sum(square + size * (off * off), axis=0, keepdims=True), whole

    mean, square, whole = combine(stat_acc)
    line = lax.broadcasted_iota(jnp.int32, (8, channels), 0)
    sent_stat[...] = jnp.where(line == 0, mean * whole, jnp.where(line == 1, square, whole))

    @pl.loop(1, n)
    def _(s):
        stat_copy(s).start()

    all_stat[me] = sent_stat[...]

    @pl.loop(1, n)
    def _(s):
        stat_copy(s).wait_recv()

    mean, square, whole = combine(all_stat)
    group_mean = group_total(mean) / group_size
    off = mean - group_mean
    group_square = group_total(square + whole * (off * off))
    mean = group_mean
    scale = gain_ref[...] * lax.rsqrt(group_square / (whole * group_size) + 1e-05)
    sides = [(r, h) for r in range(2) for h in range(channels // 128)]
    half_scale = 0.5 * scale
    half_shift = 0.5 * (bias_ref[...] - mean * scale)

    @pl.loop(0, n)
    def _(s):
        pixels = pl.ds(pl.multiple_of(s * 2 * row_tokens, 8), 2 * row_tokens)
        step = lax.rem(s, 2 * share)
        f = frame_of(lax.div(s, 2 * share) * share + lax.rem(step, share), lax.div(step, share))
        live = f < valid
        for r, h in sides:
            lanes = slice(h * 128, (h + 1) * 128)
            normed = out_buf[r, h, pixels, :] * half_scale[:, lanes] + half_shift[:, lanes]
            silu = normed + normed * jnp.tanh(normed)
            decoded_ref[f, r, :, lanes] = jnp.where(live, silu, 0.0).astype(BF16)

    @pl.loop(0, n // 2)
    def _(slot):
        @pl.when(slot != mine)
        def _():
            tok_copy(slot).wait_send()

    @pl.loop(0, chunks)
    def _(c):
        made_copy(0, c).wait_send()
        made_copy(2, c).wait_send()
        relay_copy(c).wait_send()

        @pl.when(across == 0)
        def _():
            made_copy(3, c).wait_send()

        @pl.when(exists)
        def _():
            made_copy(1, c).wait_send()

    @pl.loop(1, n)
    def _(s):
        stat_copy(s).wait_send()

    @pl.loop(1, levels)
    def _(k):
        column_copy(k).wait_send()

    @pl.loop(0, levels)
    def _(k):
        row_pass(k).wait_send()
        core_pass(k, 0).wait_send()
        core_pass(k, 1).wait_send()


def local(
    tokens,
    qkv_weight,
    out_weight,
    conv_weight,
    norm_gain,
    norm_bias,
    group_map,
    token_order,
    valid_frames,
):
    n = lax.axis_size("tm")
    count, width = tokens.shape
    channels = conv_weight.shape[3]
    row_tokens = count // n
    chunks = count // CHUNK
    share = n // (2 * chunks)
    state_shape = (width // 128 * (width // HEADS) + 16, 128)
    anywhere = pl.BlockSpec(memory_space=pltpu.HBM)
    vmem = pl.BlockSpec(memory_space=pltpu.VMEM)
    smem = pl.BlockSpec(memory_space=pltpu.SMEM)
    dma = pltpu.SemaphoreType.DMA
    return pl.pallas_call(
        functools.partial(mega, n),
        out_shape=pltpu.VMEM((n, 2, 2 * row_tokens, channels), BF16),
        in_specs=[anywhere] * 4 + [vmem, vmem, smem, vmem, smem],
        out_specs=vmem,
        scratch_shapes=[
            pltpu.VMEM((count, width), BF16),
            pltpu.VMEM((width, 3 * width), BF16),
            pltpu.VMEM((width, 4 * channels), BF16),
            pltpu.VMEM((3, 3 * channels, channels), BF16),
            pltpu.VMEM((n // 2, 2 * row_tokens, width), BF16),
            pltpu.VMEM((n // 2, 2 * row_tokens, width), BF16),
            pltpu.VMEM((width // BLOCK, BLOCK, BLOCK), F32),
            pltpu.VMEM((8, width), F32),
            pltpu.VMEM(state_shape, BF16),
            pltpu.VMEM((n,) + state_shape, BF16),
            pltpu.VMEM((n,) + state_shape, F32),
            pltpu.VMEM(state_shape, F32),
            pltpu.VMEM(state_shape, F32),
            pltpu.VMEM((count, width), F32),
            pltpu.VMEM((2, chunks, share, row_tokens, width), BF16),
            pltpu.VMEM((3, chunks, 2, share, row_tokens, width), BF16),
            pltpu.VMEM((4, CHUNK, 4 * channels), BF16),
            pltpu.VMEM((2 * chunks, 8, channels), F32),
            pltpu.VMEM((8, channels), F32),
            pltpu.VMEM((n, 8, channels), F32),
            pltpu.VMEM((2, channels // 128, 2 * count, 128), F32),
            dma((4,)),
            dma((n // 2,)),
            dma((n // 2,)),
            dma((2, n // 4)),
            dma((2, n // 4)),
            dma((n // 4,)),
            dma((n // 4,)),
            dma((n // 4,)),
            dma((n // 4,)),
            dma((4, chunks)),
            dma((chunks,)),
            dma((3, chunks, 2)),
            dma((n,)),
            dma((n,)),
        ],
        compiler_params=pltpu.CompilerParams(
            collective_id=0, has_side_effects=True, vmem_limit_bytes=VMEM - 2 * count * 4 * channels
        ),
    )(
        tokens,
        qkv_weight,
        out_weight,
        conv_weight.reshape(3, 3 * channels, channels),
        norm_gain[None],
        norm_bias[None],
        group_map,
        token_order[None],
        valid_frames,
    )


def solution(mesh):
    in_specs = (P(("clip", "tm"), None), P(), P(), P(), P(), P(), P("clip"), P("clip"), P("clip"))
    out_specs = P("clip", "tm", None, None)
    return jax.shard_map(local, mesh=mesh, in_specs=in_specs, out_specs=out_specs, check_vma=False)
```

```python
import functools

import jax
import jax.numpy as jnp
from jax import lax
from jax.experimental import pallas as pl
from jax.experimental.pallas import tpu as pltpu
from jax.sharding import PartitionSpec as P

HEADS = 16
NORM_GROUPS = 32
MESH = pl.DeviceIdType.MESH
F32 = jnp.float32
BF16 = jnp.bfloat16
CHUNK = 256
BLOCK = 256
VMEM = 66650112


def flat(cells):
    rows, width = cells.shape[-2:]
    every = cells.size // width
    if rows % 16 == 0:
        return cells.reshape(every, width)
    return cells.astype(F32).reshape(every, width).astype(BF16)


def mega(
    n,
    tokens_hbm,
    qkv_hbm,
    out_hbm,
    conv_hbm,
    gain_ref,
    bias_ref,
    group_ref,
    order_ref,
    valid_ref,
    decoded_ref,
    tokens_ref,
    qkv_ref,
    outw_ref,
    convw_ref,
    sent_tokens,
    tile_tokens,
    state_acc,
    sum_acc,
    sent_state,
    all_state,
    all_total,
    running,
    prefix,
    rows_ref,
    made,
    near_rows,
    cells,
    stat_acc,
    sent_stat,
    all_stat,
    out_buf,
    load_sem,
    tok_send,
    tok_recv,
    core_send,
    core_recv,
    col_send,
    col_recv,
    row_send,
    row_recv,
    made_send,
    relay_send,
    near_recv,
    stat_send,
    stat_recv,
):
    me = lax.axis_index("tm")
    count, width = tokens_ref.shape
    row_tokens = count // n
    pair_tokens = 2 * row_tokens
    chunks = count // CHUNK
    share = n // (2 * chunks)
    head_dim = width // HEADS
    channels = gain_ref.shape[1]
    blocks = width // BLOCK
    heads_per = BLOCK // head_dim
    group_size = channels // NORM_GROUPS

    levels = n // 4
    level = lax.div(me, 4)
    y = lax.rem(lax.div(me, 2), 2)
    core = lax.rem(me, 2)
    side = lax.div(me, n // 2)
    place = lax.div(me, n // chunks)
    inward = place + side * (chunks - 1 - 2 * place)
    inner = inward == 1
    mine = 2 * level + core
    core_peer = me + 1 - 2 * core
    row_peer = me + 2 - 4 * y

    def facing(k):
        return k + side * (chunks - 1 - 2 * k)

    def frame_of(source, column):
        return 4 * lax.div(source, 2) + 2 * column + lax.rem(source, 2)

    loads = [
        pltpu.make_async_copy(a, b, load_sem.at[i])
        for i, (a, b) in enumerate(
            [
                (tokens_hbm, tokens_ref),
                (qkv_hbm, qkv_ref),
                (out_hbm, outw_ref),
                (conv_hbm, convw_ref),
            ]
        )
    ]
    for load in loads:
        load.start()

    barrier = pltpu.get_barrier_semaphore()

    @pl.loop(1, n)
    def _(s):
        pl.semaphore_signal(
            barrier, inc=1, device_id={"tm": lax.rem(me + s, n)}, device_id_type=MESH
        )

    def remote(src, dst, send_sem, recv_sem, device):
        return pltpu.make_async_remote_copy(
            src_ref=src,
            dst_ref=dst,
            send_sem=send_sem,
            recv_sem=recv_sem,
            device_id={"tm": device},
            device_id_type=MESH,
        )

    def tok_copy(slot):
        return remote(
            sent_tokens.at[slot],
            tile_tokens.at[mine],
            tok_send.at[slot],
            tok_recv.at[mine],
            4 * lax.div(slot, 2) + 2 * y + lax.rem(slot, 2),
        )

    def tok_arrival(source):
        return remote(
            sent_tokens.at[source],
            tile_tokens.at[source],
            tok_send.at[source],
            tok_recv.at[source],
            4 * lax.div(source, 2) + 2 * y + lax.rem(source, 2),
        )

    def column_copy(k):
        return remote(
            sent_state,
            all_state.at[me],
            col_send.at[k],
            col_recv.at[k],
            lax.rem(me + 4 * k, n),
        )

    def pass_on(source, peer, send_sem, recv_sem):
        return remote(all_state.at[source], all_state.at[source], send_sem, recv_sem, peer)

    def row_pass(k):
        source = lax.rem(me + n - 4 * k, n)
        return pass_on(source, row_peer, row_send.at[k], row_recv.at[k])

    def core_pass(k, d):
        source = lax.rem(me + d * (row_peer - me) + n - 4 * k, n)
        return pass_on(source, core_peer, core_send.at[d, k], core_recv.at[d, k])

    def stat_copy(s):
        return remote(
            sent_stat,
            all_stat.at[me],
            stat_send.at[s],
            stat_recv.at[s],
            lax.rem(me + s, n),
        )

    across = lax.rem(y + core, 2)
    outer_owner = 4 * level + 3 * core
    inner_owner = 4 * level + 1 + core
    beyond = 4 * level - 1 + 5 * core
    exists = jnp.logical_and(beyond >= 0, beyond < n)
    beyond_device = jnp.clip(beyond, 0, n - 1)
    far_slot = 2 * core
    peer_slot = 2 - 2 * core

    def made_copy(kind, c):
        if kind == 0:
            part, device, slot = 1 - core, inner_owner, 1
        elif kind == 1:
            part, device, slot = core, beyond_device, peer_slot
        elif kind == 2:
            part = core
            device = across * outer_owner + (1 - across) * inner_owner
            slot = across + (1 - across) * far_slot
        else:
            part, device, slot = 1 - core, 4 * level + 2 - core, far_slot
        return remote(
            made.at[part, c],
            near_rows.at[slot, c, y],
            made_send.at[kind, c],
            near_recv.at[slot, c, y],
            device,
        )

    def relay_copy(c):
        return remote(
            near_rows.at[1, c, 1 - y],
            near_rows.at[far_slot, c, 1 - y],
            relay_send.at[c],
            near_recv.at[far_slot, c, 1 - y],
            core_peer,
        )

    def near_arrival(slot, c, column):
        return remote(
            near_rows.at[slot, c, column],
            near_rows.at[slot, c, column],
            made_send.at[0, c],
            near_recv.at[slot, c, column],
            core_peer,
        )

    loads[0].wait()

    def permute(to):
        where = lax.broadcasted_iota(jnp.int32, (CHUNK, count), 0) + to * CHUNK
        pick = jnp.where(order_ref[...] == where, 1.0, 0.0).astype(BF16)
        moved = jnp.dot(pick, tokens_ref[...], preferred_element_type=F32)
        sent_tokens[pl.ds(to * share, share)] = moved.reshape(share, pair_tokens, width).astype(
            BF16
        )

    def send_tiles(to):
        @pl.loop(0, share)
        def _(k):
            slot = to * share + k

            @pl.when(slot != mine)
            def _():
                tok_copy(slot).start()

    targets = [facing(x) for x in (inward + 1, inward * 0, 2 - inward, inward * 0 + 3)]

    loads[1].wait()
    state_acc[...] = jnp.zeros_like(state_acc)
    sum_acc[...] = jnp.zeros_like(sum_acc)

    @pl.loop(0, chunks)
    def _(c):
        rows = pl.ds(pl.multiple_of(c * CHUNK, CHUNK), CHUNK)
        mixed = jnp.dot(
            tokens_ref[rows, :], qkv_ref[:, width : 3 * width], preferred_element_type=F32
        ).astype(BF16)
        keys = jnp.maximum(mixed[:, :width], jnp.zeros((), BF16))
        sum_acc[...] += keys.astype(F32).reshape(CHUNK // 8, 8, width).sum(axis=0)
        for b in range(blocks):
            lanes = slice(b * BLOCK, (b + 1) * BLOCK)
            state_acc[b] += lax.dot_general(
                keys[:, lanes],
                mixed[:, width + b * BLOCK : width + (b + 1) * BLOCK],
                (((0,), (0,)), ((), ())),
                preferred_element_type=F32,
            )

    head_row = lax.broadcasted_iota(jnp.int32, (BLOCK, BLOCK), 0) // head_dim
    head_col = lax.broadcasted_iota(jnp.int32, (BLOCK, BLOCK), 1) // head_dim
    same_head = head_row == head_col
    pieces = width // 128
    sum_at = pieces * head_dim
    for b in range(blocks):
        own = jnp.where(same_head, state_acc[b], 0.0)
        own = own.reshape(heads_per, head_dim, BLOCK).sum(axis=0).astype(BF16)
        for i in range(BLOCK // 128):
            at = (b * (BLOCK // 128) + i) * head_dim
            sent_state[at : at + head_dim, :] = own[:, i * 128 : (i + 1) * 128]
    key_sum = jnp.sum(sum_acc[...], axis=0, keepdims=True)
    high = key_sum.astype(BF16).astype(F32)
    line = lax.broadcasted_iota(jnp.int32, (16, 128), 0)
    packed = jnp.zeros((16, 128), F32)
    for i in range(pieces):
        lanes = slice(i * 128, (i + 1) * 128)
        packed = jnp.where(line == i, high[:, lanes], packed)
        packed = jnp.where(line == pieces + i, (key_sum - high)[:, lanes], packed)
    sent_state[sum_at : sum_at + 16, :] = packed.astype(BF16)

    all_state[me] = sent_state[...]

    pl.semaphore_wait(barrier, n - 1)

    @pl.loop(1, levels)
    def _(k):
        column_copy(k).start()

    row_pass(0).start()
    core_pass(0, 0).start()

    permute(targets[0])
    send_tiles(targets[0])
    permute(targets[1])
    send_tiles(targets[1])

    @pl.loop(0, chunks // 2)
    def _(k):
        permute(facing((1 - k) * (2 - inward) + k * 3))

    tile_tokens[mine] = sent_tokens[mine]

    send_tiles(targets[2])
    send_tiles(targets[3])

    @pl.loop(1, levels)
    def _(k):
        column_copy(k).wait_recv()
        row_pass(k).start()
        core_pass(k, 0).start()

    @pl.loop(0, levels)
    def _(k):
        row_pass(k).wait_recv()
        core_pass(k, 1).start()

    def attend_order(k):
        late = lax.div(k, 2)
        return facing(
            (1 - late) * (inward + k * (1 - 2 * inward))
            + late * ((3 - k) * (3 - inward) + (k - 2) * (2 + inward))
        )

    def queries(c):
        @pl.loop(0, share)
        def _(k):
            source = c * share + k

            @pl.when(source != mine)
            def _():
                tok_arrival(source).wait_recv()

        mixed = jnp.dot(
            flat(tile_tokens[pl.ds(c * share, share)]),
            qkv_ref[:, 0:width],
            preferred_element_type=F32,
        ).astype(BF16)
        rows = pl.ds(pl.multiple_of(c * CHUNK, CHUNK), CHUNK)
        rows_ref[rows, :] = jnp.maximum(mixed, jnp.zeros((), BF16)).astype(F32)

    queries(attend_order(0))

    @pl.loop(0, levels)
    def _(k):
        core_pass(k, 0).wait_recv()
        core_pass(k, 1).wait_recv()

    running[...] = jnp.zeros_like(running)
    prefix[...] = jnp.zeros_like(prefix)

    @pl.loop(0, n)
    def _(f):
        new_group = group_ref[f] != group_ref[jnp.maximum(f - 1, 0)]
        before = jnp.where(new_group, running[...], prefix[...])
        prefix[...] = before
        own = all_state[f].astype(F32)
        running[...] += own
        all_total[f] = before + own

    head_ones = same_head.astype(F32).astype(BF16)
    reach = 3 * channels

    def attend_chunk(c):
        rows = pl.ds(pl.multiple_of(c * CHUNK, CHUNK), CHUNK)

        def attend(k, carry):
            total = all_total[frame_of(c * share + k, y)]
            key_total = jnp.concatenate(
                [
                    total[sum_at + i : sum_at + i + 1, :]
                    + total[sum_at + pieces + i : sum_at + pieces + i + 1, :]
                    for i in range(pieces)
                ],
                axis=1,
            )
            here = pl.ds(pl.multiple_of(c * CHUNK + k * pair_tokens, 16), pair_tokens)
            query = rows_ref[here, :]
            scaled = (query * key_total).astype(BF16)
            query = query.astype(BF16)
            for b in range(blocks):
                lanes = slice(b * BLOCK, (b + 1) * BLOCK)
                first = b * (BLOCK // 128)
                state = jnp.concatenate(
                    [
                        total[i * head_dim : (i + 1) * head_dim, :]
                        for i in range(first, first + BLOCK // 128)
                    ],
                    axis=1,
                )
                high = state.astype(BF16).astype(F32)
                numer = jnp.zeros((pair_tokens, BLOCK), F32)
                for part in (high, state - high):
                    spread = jnp.concatenate([part] * heads_per, axis=0)
                    spread = jnp.where(same_head, spread, 0.0).astype(BF16)
                    numer += jnp.dot(query[:, lanes], spread, preferred_element_type=F32)
                denom = jnp.dot(scaled[:, lanes], head_ones, preferred_element_type=F32) + 1.0
                rows_ref[here, lanes] = numer / denom
            return carry

        lax.fori_loop(0, share, attend, 0, unroll=share <= 4)
        attended = rows_ref[rows, :].reshape(share, 2, row_tokens, width)
        for i in range(2):
            made[i, c] = attended[:, i].astype(BF16)
        made_copy(0, c).start()
        made_copy(2, c).start()

        @pl.when(across == 0)
        def _():
            made_copy(3, c).start()

        @pl.when(across == 0)
        def _():
            near_rows[1, c, y] = made[core, c]
            near_rows[peer_slot, c, y] = made[1 - core, c]

        @pl.when(across == 1)
        def _():
            near_rows[far_slot, c, y] = made[1 - core, c]

    attend_chunk(attend_order(0))
    queries(attend_order(1))
    attend_chunk(attend_order(1))

    loads[2].wait()
    loads[3].wait()

    def widen(even, odd):
        column = lax.rem(lax.broadcasted_iota(jnp.int32, even.shape, 0), row_tokens)
        odd_left = jnp.where(column == 0, 0.0, pltpu.roll(odd, 1, 0))
        even_right = jnp.where(column == row_tokens - 1, 0.0, pltpu.roll(even, CHUNK - 1, 0))
        return [x.astype(BF16) for x in (odd_left, even, odd, even_right)]

    valid = valid_ref[me]
    valid_above = jnp.where(me > 0, valid_ref[jnp.maximum(me - 1, 0)], 0)
    valid_below = jnp.where(me < n - 1, valid_ref[jnp.minimum(me + 1, n - 1)], 0)
    valid_rows = valid * row_tokens

    outer = across == 0
    half = 2 * channels
    limits = (valid_above, valid, valid, valid_below)

    def frames_here():
        row = lax.broadcasted_iota(jnp.int32, (CHUNK, channels), 0)
        step = lax.div(row, row_tokens)
        return lax.rem(step, share), lax.div(step, share)

    def chunk_frames(c):
        k, column = frames_here()
        return frame_of(c * share + k, column)

    def place_line(p, line, frame, limit):
        live = frame < limit
        even = jnp.where(live, line[:, :channels], 0.0)
        odd = jnp.where(live, line[:, channels:], 0.0)
        for i, part in enumerate(widen(even, odd)):
            cells[p, :, i * channels : (i + 1) * channels] = part

    def out_pixels(c, b):
        return pl.ds(c * 2 * CHUNK + b, CHUNK, 2)

    def gather_stats(c, r, results, live):
        eights = [x.reshape(CHUNK // 8, 8, channels).sum(axis=0) for x in results]
        total = jnp.sum(eights[0] + eights[1], axis=0, keepdims=True)
        size = jnp.clip(valid_rows - c * CHUNK, 0, CHUNK) * 2
        centre = total / jnp.maximum(size, 1).astype(F32)
        square = jnp.zeros((8, channels), F32)
        for x in results:
            off = jnp.where(live, x - centre, 0.0)
            square += (off * off).reshape(CHUNK // 8, 8, channels).sum(axis=0)
        square = jnp.sum(square, axis=0, keepdims=True)
        line = lax.broadcasted_iota(jnp.int32, (8, channels), 0)
        stat_acc[2 * c + r] = jnp.where(
            line == 0, total, jnp.where(line == 1, square, size.astype(F32))
        )

    def relay(c):
        near_arrival(1, c, 1 - y).wait_recv()
        relay_copy(c).start()

    def decode(c, defer):
        @pl.when(jnp.logical_not(outer))
        def _():
            near_arrival(1, c, y).wait_recv()
            near_arrival(peer_slot, c, y).wait_recv()
            near_arrival(far_slot, c, 1 - y).wait_recv()

        if not defer:

            @pl.when(jnp.logical_and(outer, exists))
            def _():
                near_arrival(far_slot, c, y).wait_recv()
                near_arrival(far_slot, c, 1 - y).wait_recv()

        frame = chunk_frames(c)
        own = jnp.dot(flat(near_rows[1, c]), outw_ref[...], preferred_element_type=F32)
        place_line(1, own[:, :half], frame, valid)
        place_line(2, own[:, half:], frame, valid)
        near_arrival(peer_slot, c, 1 - y).wait_recv()
        absent = outer if defer else jnp.logical_and(outer, jnp.logical_not(exists))
        for p, slot, low in ((0, 0, half), (3, 2, 0)):
            missing = jnp.logical_and(absent, far_slot == slot)

            @pl.when(missing)
            def _():
                cells[p] = jnp.zeros(cells.shape[1:], BF16)

            @pl.when(jnp.logical_not(missing))
            def _():
                line = jnp.dot(
                    flat(near_rows[slot, c]),
                    outw_ref[:, low : low + half],
                    preferred_element_type=F32,
                )
                place_line(p, line, frame, limits[p])

        live = frame < valid
        for r in range(2):
            results = []
            for b in range(2):
                lanes = slice(b * channels, b * channels + reach)
                result = sum(
                    jnp.dot(cells[r + d, :, lanes], convw_ref[d], preferred_element_type=F32)
                    for d in range(3)
                )
                result = jnp.where(live, result, 0.0)
                results.append(result)
                for h in range(0, channels, 128):
                    out_buf[r, h // 128, out_pixels(c, b), :] = result[:, h : h + 128]
            gather_stats(c, r, results, live)

    def finish(c):
        near_arrival(far_slot, c, y).wait_recv()
        near_arrival(far_slot, c, 1 - y).wait_recv()
        frame = chunk_frames(c)
        line = jnp.dot(
            flat(near_rows[far_slot, c]),
            outw_ref[:, pl.ds(pl.multiple_of((1 - core) * half, half), half)],
            preferred_element_type=F32,
        )
        place_line(0, line, frame, jnp.where(core == 0, valid_above, valid_below))
        live = frame < valid
        results = []
        for b in range(2):
            lanes = slice(b * channels, b * channels + reach)
            result = jnp.dot(cells[0, :, lanes], convw_ref[far_slot], preferred_element_type=F32)
            before = jnp.concatenate(
                [out_buf[core, h, out_pixels(c, b), :] for h in range(channels // 128)], axis=1
            )
            result = before + jnp.where(live, result, 0.0)
            results.append(result)
            for h in range(0, channels, 128):
                out_buf[core, h // 128, out_pixels(c, b), :] = result[:, h : h + 128]
        gather_stats(c, core, results, live)

    def reach_beyond(*steps):
        @pl.when(exists)
        def _():
            for k in steps:
                made_copy(1, attend_order(k)).start()

    def first_decode():
        decode(attend_order(0), True)

    @pl.when(jnp.logical_and(inner, core == 1))
    def _():
        reach_beyond(0, 1)
        relay(attend_order(0))
        first_decode()

    @pl.when(jnp.logical_not(inner))
    def _():
        relay(attend_order(0))

    queries(attend_order(2))
    attend_chunk(attend_order(2))

    @pl.when(jnp.logical_not(jnp.logical_and(inner, core == 1)))
    def _():
        reach_beyond(0, 1)

    @pl.when(jnp.logical_not(inner))
    def _():
        first_decode()

    queries(attend_order(3))
    attend_chunk(attend_order(3))
    reach_beyond(2, 3)

    @pl.when(jnp.logical_and(inner, core == 0))
    def _():
        relay(attend_order(0))
        first_decode()

    relay(attend_order(1))

    decode(attend_order(1), True)
    relay(attend_order(2))
    decode(attend_order(2), True)

    @pl.when(jnp.logical_and(outer, exists))
    def _():
        @pl.loop(0, 3)
        def _(k):
            finish(attend_order(k))

    relay(attend_order(3))
    decode(attend_order(3), False)

    group_row = lax.broadcasted_iota(jnp.int32, (channels, channels), 0) // group_size
    group_col = lax.broadcasted_iota(jnp.int32, (channels, channels), 1) // group_size
    group_ones = jnp.where(group_row == group_col, 1.0, 0.0).astype(BF16)

    def group_total(sums):
        parts = []
        for _ in range(3):
            part = sums.astype(BF16)
            parts.append(part)
            sums = sums - part.astype(F32)
        line = lax.broadcasted_iota(jnp.int32, (16, channels), 0)
        stacked = jnp.zeros((16, channels), F32)
        for i, part in enumerate(parts):
            stacked = jnp.where(line == i, part.astype(F32), stacked)
        found = jnp.dot(stacked.astype(BF16), group_ones, preferred_element_type=F32)
        return found[0:1] + found[1:2] + found[2:3]

    def combine(total, square, size):
        whole = jnp.sum(size, axis=0, keepdims=True)
        mean = jnp.sum(total, axis=0, keepdims=True) / whole
        off = total / jnp.maximum(size, 1.0) - mean
        return mean, jnp.sum(square + size * (off * off), axis=0, keepdims=True), whole

    mean, square, whole = combine(*[stat_acc[:, i, :] for i in range(3)])
    halves = channels // 128
    line = lax.broadcasted_iota(jnp.int32, (8, 128), 0)
    packed = jnp.zeros((8, 128), F32)
    for i, field in enumerate((mean * whole, square, whole)):
        for h in range(halves):
            packed = jnp.where(line == i * halves + h, field[:, h * 128 : (h + 1) * 128], packed)
    sent_stat[...] = packed

    @pl.loop(1, n)
    def _(s):
        stat_copy(s + (1 - side) * (n - 2 * s)).start()

    all_stat[me] = sent_stat[...]

    @pl.loop(1, n)
    def _(s):
        stat_copy(s).wait_recv()

    mean, square, whole = combine(
        *[
            jnp.concatenate([all_stat[:, i * halves + h, :] for h in range(halves)], axis=1)
            for i in range(3)
        ]
    )
    group_mean = group_total(mean) / group_size
    off = mean - group_mean
    group_square = group_total(square + whole * (off * off))
    mean = group_mean
    scale = gain_ref[...] * lax.rsqrt(group_square / (whole * group_size) + 1e-05)
    sides = [(r, h) for r in range(2) for h in range(channels // 128)]
    half_scale = 0.5 * scale
    half_shift = 0.5 * (bias_ref[...] - mean * scale)

    @pl.loop(0, n)
    def _(s):
        pixels = pl.ds(pl.multiple_of(s * 2 * row_tokens, 8), 2 * row_tokens)
        step = lax.rem(s, 2 * share)
        f = frame_of(lax.div(s, 2 * share) * share + lax.rem(step, share), lax.div(step, share))
        live = f < valid
        for r, h in sides:
            lanes = slice(h * 128, (h + 1) * 128)
            normed = out_buf[r, h, pixels, :] * half_scale[:, lanes] + half_shift[:, lanes]
            silu = normed + normed * jnp.tanh(normed)
            decoded_ref[f, r, :, lanes] = jnp.where(live, silu, 0.0).astype(BF16)

    @pl.loop(0, n // 2)
    def _(slot):
        @pl.when(slot != mine)
        def _():
            tok_copy(slot).wait_send()

    @pl.loop(0, chunks)
    def _(c):
        made_copy(0, c).wait_send()
        made_copy(2, c).wait_send()
        relay_copy(c).wait_send()

        @pl.when(across == 0)
        def _():
            made_copy(3, c).wait_send()

        @pl.when(exists)
        def _():
            made_copy(1, c).wait_send()

    @pl.loop(1, n)
    def _(s):
        stat_copy(s).wait_send()

    @pl.loop(1, levels)
    def _(k):
        column_copy(k).wait_send()

    @pl.loop(0, levels)
    def _(k):
        row_pass(k).wait_send()
        core_pass(k, 0).wait_send()
        core_pass(k, 1).wait_send()


def local(
    tokens,
    qkv_weight,
    out_weight,
    conv_weight,
    norm_gain,
    norm_bias,
    group_map,
    token_order,
    valid_frames,
):
    n = lax.axis_size("tm")
    count, width = tokens.shape
    channels = conv_weight.shape[3]
    row_tokens = count // n
    chunks = count // CHUNK
    share = n // (2 * chunks)
    state_shape = (width // 128 * (width // HEADS) + 16, 128)
    anywhere = pl.BlockSpec(memory_space=pltpu.HBM)
    vmem = pl.BlockSpec(memory_space=pltpu.VMEM)
    smem = pl.BlockSpec(memory_space=pltpu.SMEM)
    dma = pltpu.SemaphoreType.DMA
    return pl.pallas_call(
        functools.partial(mega, n),
        out_shape=pltpu.VMEM((n, 2, 2 * row_tokens, channels), BF16),
        in_specs=[anywhere] * 4 + [vmem, vmem, smem, vmem, smem],
        out_specs=vmem,
        scratch_shapes=[
            pltpu.VMEM((count, width), BF16),
            pltpu.VMEM((width, 3 * width), BF16),
            pltpu.VMEM((width, 4 * channels), BF16),
            pltpu.VMEM((3, 3 * channels, channels), BF16),
            pltpu.VMEM((n // 2, 2 * row_tokens, width), BF16),
            pltpu.VMEM((n // 2, 2 * row_tokens, width), BF16),
            pltpu.VMEM((width // BLOCK, BLOCK, BLOCK), F32),
            pltpu.VMEM((8, width), F32),
            pltpu.VMEM(state_shape, BF16),
            pltpu.VMEM((n,) + state_shape, BF16),
            pltpu.VMEM((n,) + state_shape, F32),
            pltpu.VMEM(state_shape, F32),
            pltpu.VMEM(state_shape, F32),
            pltpu.VMEM((count, width), F32),
            pltpu.VMEM((2, chunks, share, row_tokens, width), BF16),
            pltpu.VMEM((3, chunks, 2, share, row_tokens, width), BF16),
            pltpu.VMEM((4, CHUNK, 4 * channels), BF16),
            pltpu.VMEM((2 * chunks, 8, channels), F32),
            pltpu.VMEM((8, 128), F32),
            pltpu.VMEM((n, 8, 128), F32),
            pltpu.VMEM((2, channels // 128, 2 * count, 128), F32),
            dma((4,)),
            dma((n // 2,)),
            dma((n // 2,)),
            dma((2, n // 4)),
            dma((2, n // 4)),
            dma((n // 4,)),
            dma((n // 4,)),
            dma((n // 4,)),
            dma((n // 4,)),
            dma((4, chunks)),
            dma((chunks,)),
            dma((3, chunks, 2)),
            dma((n,)),
            dma((n,)),
        ],
        compiler_params=pltpu.CompilerParams(
            collective_id=0, has_side_effects=True, vmem_limit_bytes=VMEM - 2 * count * 4 * channels
        ),
    )(
        tokens,
        qkv_weight,
        out_weight,
        conv_weight.reshape(3, 3 * channels, channels),
        norm_gain[None],
        norm_bias[None],
        group_map,
        token_order[None],
        valid_frames,
    )


def solution(mesh):
    in_specs = (P(("clip", "tm"), None), P(), P(), P(), P(), P(), P("clip"), P("clip"), P("clip"))
    out_specs = P("clip", "tm", None, None)
    return jax.shard_map(local, mesh=mesh, in_specs=in_specs, out_specs=out_specs, check_vma=False)
```

```python
import functools

import jax
import jax.numpy as jnp
from jax import lax
from jax.experimental import pallas as pl
from jax.experimental.pallas import tpu as pltpu
from jax.sharding import PartitionSpec as P

HEADS = 16
NORM_GROUPS = 32
MESH = pl.DeviceIdType.MESH
F32 = jnp.float32
BF16 = jnp.bfloat16
CHUNK = 256
BLOCK = 256
VMEM = 66650112


def flat(cells):
    rows, width = cells.shape[-2:]
    every = cells.size // width
    if rows % 16 == 0:
        return cells.reshape(every, width)
    return cells.astype(F32).reshape(every, width).astype(BF16)


def mega(
    n,
    tokens_hbm,
    qkv_hbm,
    out_hbm,
    conv_hbm,
    gain_ref,
    bias_ref,
    group_ref,
    order_ref,
    valid_ref,
    decoded_ref,
    tokens_ref,
    qkv_ref,
    outw_ref,
    convw_ref,
    sent_tokens,
    tile_tokens,
    state_acc,
    sum_acc,
    sent_state,
    all_state,
    all_total,
    running,
    prefix,
    rows_ref,
    made,
    near_rows,
    cells,
    stat_acc,
    sent_stat,
    all_stat,
    out_buf,
    load_sem,
    tok_send,
    tok_recv,
    core_send,
    core_recv,
    col_send,
    col_recv,
    row_send,
    row_recv,
    made_send,
    relay_send,
    near_recv,
    stat_send,
    stat_recv,
):
    me = lax.axis_index("tm")
    count, width = tokens_ref.shape
    row_tokens = count // n
    pair_tokens = 2 * row_tokens
    chunks = count // CHUNK
    share = n // (2 * chunks)
    head_dim = width // HEADS
    channels = gain_ref.shape[1]
    blocks = width // BLOCK
    heads_per = BLOCK // head_dim
    group_size = channels // NORM_GROUPS

    levels = n // 4
    level = lax.div(me, 4)
    y = lax.rem(lax.div(me, 2), 2)
    core = lax.rem(me, 2)
    side = lax.div(me, n // 2)
    place = lax.div(me, n // chunks)
    inward = place + side * (chunks - 1 - 2 * place)
    inner = inward == 1
    mine = 2 * level + core
    core_peer = me + 1 - 2 * core
    row_peer = me + 2 - 4 * y

    def facing(k):
        return k + side * (chunks - 1 - 2 * k)

    def frame_of(source, column):
        return 4 * lax.div(source, 2) + 2 * column + lax.rem(source, 2)

    loads = [
        pltpu.make_async_copy(a, b, load_sem.at[i])
        for i, (a, b) in enumerate(
            [
                (tokens_hbm, tokens_ref),
                (qkv_hbm, qkv_ref),
                (out_hbm, outw_ref),
                (conv_hbm, convw_ref),
            ]
        )
    ]
    for load in loads:
        load.start()

    barrier = pltpu.get_barrier_semaphore()

    @pl.loop(1, n)
    def _(s):
        pl.semaphore_signal(
            barrier, inc=1, device_id={"tm": lax.rem(me + s, n)}, device_id_type=MESH
        )

    def remote(src, dst, send_sem, recv_sem, device):
        return pltpu.make_async_remote_copy(
            src_ref=src,
            dst_ref=dst,
            send_sem=send_sem,
            recv_sem=recv_sem,
            device_id={"tm": device},
            device_id_type=MESH,
        )

    def tok_copy(slot):
        return remote(
            sent_tokens.at[slot],
            tile_tokens.at[mine],
            tok_send.at[slot],
            tok_recv.at[mine],
            4 * lax.div(slot, 2) + 2 * y + lax.rem(slot, 2),
        )

    def tok_arrival(source):
        return remote(
            sent_tokens.at[source],
            tile_tokens.at[source],
            tok_send.at[source],
            tok_recv.at[source],
            4 * lax.div(source, 2) + 2 * y + lax.rem(source, 2),
        )

    def column_copy(k):
        return remote(
            sent_state,
            all_state.at[me],
            col_send.at[k],
            col_recv.at[k],
            lax.rem(me + 4 * k, n),
        )

    def pass_on(source, peer, send_sem, recv_sem):
        return remote(all_state.at[source], all_state.at[source], send_sem, recv_sem, peer)

    def row_pass(k):
        source = lax.rem(me + n - 4 * k, n)
        return pass_on(source, row_peer, row_send.at[k], row_recv.at[k])

    def core_pass(k, d):
        source = lax.rem(me + d * (row_peer - me) + n - 4 * k, n)
        return pass_on(source, core_peer, core_send.at[d, k], core_recv.at[d, k])

    def stat_copy(s):
        return remote(
            sent_stat,
            all_stat.at[me],
            stat_send.at[s],
            stat_recv.at[s],
            lax.rem(me + s, n),
        )

    across = lax.rem(y + core, 2)
    outer_owner = 4 * level + 3 * core
    inner_owner = 4 * level + 1 + core
    beyond = 4 * level - 1 + 5 * core
    exists = jnp.logical_and(beyond >= 0, beyond < n)
    beyond_device = jnp.clip(beyond, 0, n - 1)
    far_slot = 2 * core
    peer_slot = 2 - 2 * core

    def made_copy(kind, c):
        if kind == 0:
            part, device, slot = 1 - core, inner_owner, 1
        elif kind == 1:
            part, device, slot = core, beyond_device, peer_slot
        elif kind == 2:
            part = core
            device = across * outer_owner + (1 - across) * inner_owner
            slot = across + (1 - across) * far_slot
        else:
            part, device, slot = 1 - core, 4 * level + 2 - core, far_slot
        return remote(
            made.at[part, c],
            near_rows.at[slot, c, y],
            made_send.at[kind, c],
            near_recv.at[slot, c, y],
            device,
        )

    def relay_copy(c):
        return remote(
            near_rows.at[1, c, 1 - y],
            near_rows.at[far_slot, c, 1 - y],
            relay_send.at[c],
            near_recv.at[far_slot, c, 1 - y],
            core_peer,
        )

    def near_arrival(slot, c, column):
        return remote(
            near_rows.at[slot, c, column],
            near_rows.at[slot, c, column],
            made_send.at[0, c],
            near_recv.at[slot, c, column],
            core_peer,
        )

    loads[0].wait()

    def permute(to):
        where = lax.broadcasted_iota(jnp.int32, (CHUNK, count), 0) + to * CHUNK
        pick = jnp.where(order_ref[...] == where, 1.0, 0.0).astype(BF16)
        moved = jnp.dot(pick, tokens_ref[...], preferred_element_type=F32)
        sent_tokens[pl.ds(to * share, share)] = moved.reshape(share, pair_tokens, width).astype(
            BF16
        )

    def send_tiles(to):
        @pl.loop(0, share)
        def _(k):
            slot = to * share + k

            @pl.when(slot != mine)
            def _():
                tok_copy(slot).start()

    targets = [facing(x) for x in (inward + 1, inward * 0, 2 - inward, inward * 0 + 3)]

    loads[1].wait()
    state_acc[...] = jnp.zeros_like(state_acc)
    sum_acc[...] = jnp.zeros_like(sum_acc)

    @pl.loop(0, chunks)
    def _(c):
        rows = pl.ds(pl.multiple_of(c * CHUNK, CHUNK), CHUNK)
        mixed = jnp.dot(
            tokens_ref[rows, :], qkv_ref[:, width : 3 * width], preferred_element_type=F32
        ).astype(BF16)
        keys = jnp.maximum(mixed[:, :width], jnp.zeros((), BF16))
        sum_acc[...] += keys.astype(F32).reshape(CHUNK // 8, 8, width).sum(axis=0)
        for b in range(blocks):
            lanes = slice(b * BLOCK, (b + 1) * BLOCK)
            state_acc[b] += lax.dot_general(
                keys[:, lanes],
                mixed[:, width + b * BLOCK : width + (b + 1) * BLOCK],
                (((0,), (0,)), ((), ())),
                preferred_element_type=F32,
            )

    head_row = lax.broadcasted_iota(jnp.int32, (BLOCK, BLOCK), 0) // head_dim
    head_col = lax.broadcasted_iota(jnp.int32, (BLOCK, BLOCK), 1) // head_dim
    same_head = head_row == head_col
    pieces = width // 128
    sum_at = pieces * head_dim
    for b in range(blocks):
        own = jnp.where(same_head, state_acc[b], 0.0)
        own = own.reshape(heads_per, head_dim, BLOCK).sum(axis=0).astype(BF16)
        for i in range(BLOCK // 128):
            at = (b * (BLOCK // 128) + i) * head_dim
            sent_state[at : at + head_dim, :] = own[:, i * 128 : (i + 1) * 128]
    key_sum = jnp.sum(sum_acc[...], axis=0, keepdims=True)
    high = key_sum.astype(BF16).astype(F32)
    line = lax.broadcasted_iota(jnp.int32, (16, 128), 0)
    packed = jnp.zeros((16, 128), F32)
    for i in range(pieces):
        lanes = slice(i * 128, (i + 1) * 128)
        packed = jnp.where(line == i, high[:, lanes], packed)
        packed = jnp.where(line == pieces + i, (key_sum - high)[:, lanes], packed)
    sent_state[sum_at : sum_at + 16, :] = packed.astype(BF16)

    all_state[me] = sent_state[...]

    pl.semaphore_wait(barrier, n - 1)

    @pl.loop(1, levels)
    def _(k):
        column_copy(k).start()

    row_pass(0).start()
    core_pass(0, 0).start()

    permute(targets[0])
    send_tiles(targets[0])
    permute(targets[1])
    send_tiles(targets[1])

    @pl.loop(0, chunks // 2)
    def _(k):
        permute(facing((1 - k) * (2 - inward) + k * 3))

    tile_tokens[mine] = sent_tokens[mine]

    send_tiles(targets[2])
    send_tiles(targets[3])

    @pl.loop(1, levels)
    def _(k):
        column_copy(k).wait_recv()
        row_pass(k).start()
        core_pass(k, 0).start()

    @pl.loop(0, levels)
    def _(k):
        row_pass(k).wait_recv()
        core_pass(k, 1).start()

    def attend_order(k):
        late = lax.div(k, 2)
        return facing(
            (1 - late) * (inward + k * (1 - 2 * inward))
            + late * ((3 - k) * (3 - inward) + (k - 2) * (2 + inward))
        )

    def queries(c):
        @pl.loop(0, share)
        def _(k):
            source = c * share + k

            @pl.when(source != mine)
            def _():
                tok_arrival(source).wait_recv()

        mixed = jnp.dot(
            flat(tile_tokens[pl.ds(c * share, share)]),
            qkv_ref[:, 0:width],
            preferred_element_type=F32,
        ).astype(BF16)
        rows = pl.ds(pl.multiple_of(c * CHUNK, CHUNK), CHUNK)
        rows_ref[rows, :] = jnp.maximum(mixed, jnp.zeros((), BF16)).astype(F32)

    queries(attend_order(0))

    @pl.loop(0, levels)
    def _(k):
        core_pass(k, 0).wait_recv()
        core_pass(k, 1).wait_recv()

    running[...] = jnp.zeros_like(running)
    prefix[...] = jnp.zeros_like(prefix)

    @pl.loop(0, n)
    def _(f):
        new_group = group_ref[f] != group_ref[jnp.maximum(f - 1, 0)]
        before = jnp.where(new_group, running[...], prefix[...])
        prefix[...] = before
        own = all_state[f].astype(F32)
        running[...] += own
        all_total[f] = before + own

    head_ones = same_head.astype(F32).astype(BF16)
    reach = 3 * channels

    def attend_chunk(c):
        rows = pl.ds(pl.multiple_of(c * CHUNK, CHUNK), CHUNK)

        def attend(k, carry):
            total = all_total[frame_of(c * share + k, y)]
            key_total = jnp.concatenate(
                [
                    total[sum_at + i : sum_at + i + 1, :]
                    + total[sum_at + pieces + i : sum_at + pieces + i + 1, :]
                    for i in range(pieces)
                ],
                axis=1,
            )
            here = pl.ds(pl.multiple_of(c * CHUNK + k * pair_tokens, 16), pair_tokens)
            query = rows_ref[here, :]
            scaled = (query * key_total).astype(BF16)
            query = query.astype(BF16)
            for b in range(blocks):
                lanes = slice(b * BLOCK, (b + 1) * BLOCK)
                first = b * (BLOCK // 128)
                state = jnp.concatenate(
                    [
                        total[i * head_dim : (i + 1) * head_dim, :]
                        for i in range(first, first + BLOCK // 128)
                    ],
                    axis=1,
                )
                high = state.astype(BF16).astype(F32)
                numer = jnp.zeros((pair_tokens, BLOCK), F32)
                for part in (high, state - high):
                    spread = jnp.concatenate([part] * heads_per, axis=0)
                    spread = jnp.where(same_head, spread, 0.0).astype(BF16)
                    numer += jnp.dot(query[:, lanes], spread, preferred_element_type=F32)
                denom = jnp.dot(scaled[:, lanes], head_ones, preferred_element_type=F32) + 1.0
                rows_ref[here, lanes] = numer / denom
            return carry

        lax.fori_loop(0, share, attend, 0, unroll=share <= 4)
        attended = rows_ref[rows, :].reshape(share, 2, row_tokens, width)
        for i in range(2):
            made[i, c] = attended[:, i].astype(BF16)
        made_copy(0, c).start()
        made_copy(2, c).start()

        @pl.when(across == 0)
        def _():
            made_copy(3, c).start()

        @pl.when(across == 0)
        def _():
            near_rows[1, c, y] = made[core, c]
            near_rows[peer_slot, c, y] = made[1 - core, c]

        @pl.when(across == 1)
        def _():
            near_rows[far_slot, c, y] = made[1 - core, c]

    attend_chunk(attend_order(0))
    queries(attend_order(1))
    attend_chunk(attend_order(1))

    loads[2].wait()
    loads[3].wait()

    def widen(even, odd):
        column = lax.rem(lax.broadcasted_iota(jnp.int32, even.shape, 0), row_tokens)
        odd_left = jnp.where(column == 0, 0.0, pltpu.roll(odd, 1, 0))
        even_right = jnp.where(column == row_tokens - 1, 0.0, pltpu.roll(even, CHUNK - 1, 0))
        return [x.astype(BF16) for x in (odd_left, even, odd, even_right)]

    valid = valid_ref[me]
    valid_above = jnp.where(me > 0, valid_ref[jnp.maximum(me - 1, 0)], 0)
    valid_below = jnp.where(me < n - 1, valid_ref[jnp.minimum(me + 1, n - 1)], 0)
    valid_rows = valid * row_tokens

    outer = across == 0
    half = 2 * channels
    limits = (valid_above, valid, valid, valid_below)

    def frames_here():
        row = lax.broadcasted_iota(jnp.int32, (CHUNK, channels), 0)
        step = lax.div(row, row_tokens)
        return lax.rem(step, share), lax.div(step, share)

    def chunk_frames(c):
        k, column = frames_here()
        return frame_of(c * share + k, column)

    def place_line(p, line, frame, limit):
        live = frame < limit
        even = jnp.where(live, line[:, :channels], 0.0)
        odd = jnp.where(live, line[:, channels:], 0.0)
        for i, part in enumerate(widen(even, odd)):
            cells[p, :, i * channels : (i + 1) * channels] = part

    def out_pixels(c, b):
        return pl.ds(c * 2 * CHUNK + b, CHUNK, 2)

    def gather_stats(c, r, results, live):
        eights = [x.reshape(CHUNK // 8, 8, channels).sum(axis=0) for x in results]
        total = jnp.sum(eights[0] + eights[1], axis=0, keepdims=True)
        size = jnp.clip(valid_rows - c * CHUNK, 0, CHUNK) * 2
        centre = total / jnp.maximum(size, 1).astype(F32)
        square = jnp.zeros((8, channels), F32)
        for x in results:
            off = jnp.where(live, x - centre, 0.0)
            square += (off * off).reshape(CHUNK // 8, 8, channels).sum(axis=0)
        square = jnp.sum(square, axis=0, keepdims=True)
        line = lax.broadcasted_iota(jnp.int32, (8, channels), 0)
        stat_acc[2 * c + r] = jnp.where(
            line == 0, total, jnp.where(line == 1, square, size.astype(F32))
        )

    def relay(c):
        near_arrival(1, c, 1 - y).wait_recv()
        relay_copy(c).start()

    def decode(c, defer):
        @pl.when(jnp.logical_not(outer))
        def _():
            near_arrival(1, c, y).wait_recv()
            near_arrival(peer_slot, c, y).wait_recv()
            near_arrival(far_slot, c, 1 - y).wait_recv()

        if not defer:

            @pl.when(jnp.logical_and(outer, exists))
            def _():
                near_arrival(far_slot, c, y).wait_recv()
                near_arrival(far_slot, c, 1 - y).wait_recv()

        frame = chunk_frames(c)
        own = jnp.dot(flat(near_rows[1, c]), outw_ref[...], preferred_element_type=F32)
        place_line(1, own[:, :half], frame, valid)
        place_line(2, own[:, half:], frame, valid)
        near_arrival(peer_slot, c, 1 - y).wait_recv()
        absent = outer if defer else jnp.logical_and(outer, jnp.logical_not(exists))
        for p, slot, low in ((0, 0, half), (3, 2, 0)):
            missing = jnp.logical_and(absent, far_slot == slot)

            @pl.when(missing)
            def _():
                cells[p] = jnp.zeros(cells.shape[1:], BF16)

            @pl.when(jnp.logical_not(missing))
            def _():
                line = jnp.dot(
                    flat(near_rows[slot, c]),
                    outw_ref[:, low : low + half],
                    preferred_element_type=F32,
                )
                place_line(p, line, frame, limits[p])

        live = frame < valid
        for r in range(2):
            results = []
            for b in range(2):
                lanes = slice(b * channels, b * channels + reach)
                result = sum(
                    jnp.dot(cells[r + d, :, lanes], convw_ref[d], preferred_element_type=F32)
                    for d in range(3)
                )
                result = jnp.where(live, result, 0.0)
                results.append(result)
                for h in range(0, channels, 128):
                    out_buf[r, h // 128, out_pixels(c, b), :] = result[:, h : h + 128]
            gather_stats(c, r, results, live)

    def finish(c):
        near_arrival(far_slot, c, y).wait_recv()
        near_arrival(far_slot, c, 1 - y).wait_recv()
        frame = chunk_frames(c)
        line = jnp.dot(
            flat(near_rows[far_slot, c]),
            outw_ref[:, pl.ds(pl.multiple_of((1 - core) * half, half), half)],
            preferred_element_type=F32,
        )
        place_line(0, line, frame, jnp.where(core == 0, valid_above, valid_below))
        live = frame < valid
        results = []
        for b in range(2):
            lanes = slice(b * channels, b * channels + reach)
            result = jnp.dot(cells[0, :, lanes], convw_ref[far_slot], preferred_element_type=F32)
            before = jnp.concatenate(
                [out_buf[core, h, out_pixels(c, b), :] for h in range(channels // 128)], axis=1
            )
            result = before + jnp.where(live, result, 0.0)
            results.append(result)
            for h in range(0, channels, 128):
                out_buf[core, h // 128, out_pixels(c, b), :] = result[:, h : h + 128]
        gather_stats(c, core, results, live)

    def reach_beyond(*steps):
        @pl.when(exists)
        def _():
            for k in steps:
                made_copy(1, attend_order(k)).start()

    def first_decode():
        decode(attend_order(0), True)

    @pl.when(jnp.logical_and(inner, core == 1))
    def _():
        reach_beyond(0, 1)
        relay(attend_order(0))
        first_decode()

    @pl.when(jnp.logical_not(inner))
    def _():
        relay(attend_order(0))

    queries(attend_order(2))
    attend_chunk(attend_order(2))

    @pl.when(jnp.logical_not(jnp.logical_and(inner, core == 1)))
    def _():
        reach_beyond(0, 1)

    @pl.when(jnp.logical_not(inner))
    def _():
        first_decode()

    queries(attend_order(3))
    attend_chunk(attend_order(3))
    reach_beyond(2, 3)

    @pl.when(jnp.logical_and(inner, core == 0))
    def _():
        relay(attend_order(0))
        first_decode()

    relay(attend_order(1))

    decode(attend_order(1), True)
    relay(attend_order(2))
    decode(attend_order(2), True)

    @pl.when(jnp.logical_and(outer, exists))
    def _():
        @pl.loop(0, 2)
        def _(k):
            finish(attend_order(k))

    relay(attend_order(3))

    @pl.when(jnp.logical_and(outer, exists))
    def _():
        finish(attend_order(2))

    decode(attend_order(3), False)

    group_row = lax.broadcasted_iota(jnp.int32, (channels, channels), 0) // group_size
    group_col = lax.broadcasted_iota(jnp.int32, (channels, channels), 1) // group_size
    group_ones = jnp.where(group_row == group_col, 1.0, 0.0).astype(BF16)

    def group_total(sums):
        parts = []
        for _ in range(3):
            part = sums.astype(BF16)
            parts.append(part)
            sums = sums - part.astype(F32)
        line = lax.broadcasted_iota(jnp.int32, (16, channels), 0)
        stacked = jnp.zeros((16, channels), F32)
        for i, part in enumerate(parts):
            stacked = jnp.where(line == i, part.astype(F32), stacked)
        found = jnp.dot(stacked.astype(BF16), group_ones, preferred_element_type=F32)
        return found[0:1] + found[1:2] + found[2:3]

    def combine(total, square, size):
        whole = jnp.sum(size, axis=0, keepdims=True)
        mean = jnp.sum(total, axis=0, keepdims=True) / whole
        off = total / jnp.maximum(size, 1.0) - mean
        return mean, jnp.sum(square + size * (off * off), axis=0, keepdims=True), whole

    mean, square, whole = combine(*[stat_acc[:, i, :] for i in range(3)])
    halves = channels // 128
    line = lax.broadcasted_iota(jnp.int32, (8, 128), 0)
    packed = jnp.zeros((8, 128), F32)
    for i, field in enumerate((mean * whole, square, whole)):
        for h in range(halves):
            packed = jnp.where(line == i * halves + h, field[:, h * 128 : (h + 1) * 128], packed)
    sent_stat[...] = packed

    @pl.loop(1, n)
    def _(s):
        stat_copy(s + (1 - side) * (n - 2 * s)).start()

    all_stat[me] = sent_stat[...]

    @pl.loop(1, n)
    def _(s):
        stat_copy(s).wait_recv()

    mean, square, whole = combine(
        *[
            jnp.concatenate([all_stat[:, i * halves + h, :] for h in range(halves)], axis=1)
            for i in range(3)
        ]
    )
    group_mean = group_total(mean) / group_size
    off = mean - group_mean
    group_square = group_total(square + whole * (off * off))
    mean = group_mean
    scale = gain_ref[...] * lax.rsqrt(group_square / (whole * group_size) + 1e-05)
    sides = [(r, h) for r in range(2) for h in range(channels // 128)]
    half_scale = 0.5 * scale
    half_shift = 0.5 * (bias_ref[...] - mean * scale)

    @pl.loop(0, n)
    def _(s):
        pixels = pl.ds(pl.multiple_of(s * 2 * row_tokens, 8), 2 * row_tokens)
        step = lax.rem(s, 2 * share)
        f = frame_of(lax.div(s, 2 * share) * share + lax.rem(step, share), lax.div(step, share))
        live = f < valid
        for r, h in sides:
            lanes = slice(h * 128, (h + 1) * 128)
            normed = out_buf[r, h, pixels, :] * half_scale[:, lanes] + half_shift[:, lanes]
            silu = normed + normed * jnp.tanh(normed)
            decoded_ref[f, r, :, lanes] = jnp.where(live, silu, 0.0).astype(BF16)

    @pl.loop(0, n // 2)
    def _(slot):
        @pl.when(slot != mine)
        def _():
            tok_copy(slot).wait_send()

    @pl.loop(0, chunks)
    def _(c):
        made_copy(0, c).wait_send()
        made_copy(2, c).wait_send()
        relay_copy(c).wait_send()

        @pl.when(across == 0)
        def _():
            made_copy(3, c).wait_send()

        @pl.when(exists)
        def _():
            made_copy(1, c).wait_send()

    @pl.loop(1, n)
    def _(s):
        stat_copy(s).wait_send()

    @pl.loop(1, levels)
    def _(k):
        column_copy(k).wait_send()

    @pl.loop(0, levels)
    def _(k):
        row_pass(k).wait_send()
        core_pass(k, 0).wait_send()
        core_pass(k, 1).wait_send()


def local(
    tokens,
    qkv_weight,
    out_weight,
    conv_weight,
    norm_gain,
    norm_bias,
    group_map,
    token_order,
    valid_frames,
):
    n = lax.axis_size("tm")
    count, width = tokens.shape
    channels = conv_weight.shape[3]
    row_tokens = count // n
    chunks = count // CHUNK
    share = n // (2 * chunks)
    state_shape = (width // 128 * (width // HEADS) + 16, 128)
    anywhere = pl.BlockSpec(memory_space=pltpu.HBM)
    vmem = pl.BlockSpec(memory_space=pltpu.VMEM)
    smem = pl.BlockSpec(memory_space=pltpu.SMEM)
    dma = pltpu.SemaphoreType.DMA
    return pl.pallas_call(
        functools.partial(mega, n),
        out_shape=pltpu.VMEM((n, 2, 2 * row_tokens, channels), BF16),
        in_specs=[anywhere] * 4 + [vmem, vmem, smem, vmem, smem],
        out_specs=vmem,
        scratch_shapes=[
            pltpu.VMEM((count, width), BF16),
            pltpu.VMEM((width, 3 * width), BF16),
            pltpu.VMEM((width, 4 * channels), BF16),
            pltpu.VMEM((3, 3 * channels, channels), BF16),
            pltpu.VMEM((n // 2, 2 * row_tokens, width), BF16),
            pltpu.VMEM((n // 2, 2 * row_tokens, width), BF16),
            pltpu.VMEM((width // BLOCK, BLOCK, BLOCK), F32),
            pltpu.VMEM((8, width), F32),
            pltpu.VMEM(state_shape, BF16),
            pltpu.VMEM((n,) + state_shape, BF16),
            pltpu.VMEM((n,) + state_shape, F32),
            pltpu.VMEM(state_shape, F32),
            pltpu.VMEM(state_shape, F32),
            pltpu.VMEM((count, width), F32),
            pltpu.VMEM((2, chunks, share, row_tokens, width), BF16),
            pltpu.VMEM((3, chunks, 2, share, row_tokens, width), BF16),
            pltpu.VMEM((4, CHUNK, 4 * channels), BF16),
            pltpu.VMEM((2 * chunks, 8, channels), F32),
            pltpu.VMEM((8, 128), F32),
            pltpu.VMEM((n, 8, 128), F32),
            pltpu.VMEM((2, channels // 128, 2 * count, 128), F32),
            dma((4,)),
            dma((n // 2,)),
            dma((n // 2,)),
            dma((2, n // 4)),
            dma((2, n // 4)),
            dma((n // 4,)),
            dma((n // 4,)),
            dma((n // 4,)),
            dma((n // 4,)),
            dma((4, chunks)),
            dma((chunks,)),
            dma((3, chunks, 2)),
            dma((n,)),
            dma((n,)),
        ],
        compiler_params=pltpu.CompilerParams(
            collective_id=0, has_side_effects=True, vmem_limit_bytes=VMEM - 2 * count * 4 * channels
        ),
    )(
        tokens,
        qkv_weight,
        out_weight,
        conv_weight.reshape(3, 3 * channels, channels),
        norm_gain[None],
        norm_bias[None],
        group_map,
        token_order[None],
        valid_frames,
    )


def solution(mesh):
    in_specs = (P(("clip", "tm"), None), P(), P(), P(), P(), P(), P("clip"), P("clip"), P("clip"))
    out_specs = P("clip", "tm", None, None)
    return jax.shard_map(local, mesh=mesh, in_specs=in_specs, out_specs=out_specs, check_vma=False)
```

```python
import functools

import jax
import jax.numpy as jnp
from jax import lax
from jax.experimental import pallas as pl
from jax.experimental.pallas import tpu as pltpu
from jax.sharding import PartitionSpec as P

HEADS = 16
NORM_GROUPS = 32
MESH = pl.DeviceIdType.MESH
F32 = jnp.float32
BF16 = jnp.bfloat16
CHUNK = 256
BLOCK = 256
VMEM = 66650112


def flat(cells):
    rows, width = cells.shape[-2:]
    every = cells.size // width
    if rows % 16 == 0:
        return cells.reshape(every, width)
    return cells.astype(F32).reshape(every, width).astype(BF16)


def mega(
    n,
    tokens_hbm,
    qkv_hbm,
    out_hbm,
    conv_hbm,
    gain_ref,
    bias_ref,
    group_ref,
    order_ref,
    valid_ref,
    decoded_ref,
    tokens_ref,
    qkv_ref,
    outw_ref,
    convw_ref,
    sent_tokens,
    tile_tokens,
    state_acc,
    sum_acc,
    sent_state,
    all_state,
    all_total,
    running,
    prefix,
    rows_ref,
    made,
    near_rows,
    cells,
    stat_acc,
    sent_stat,
    all_stat,
    out_buf,
    load_sem,
    tok_send,
    tok_recv,
    core_send,
    core_recv,
    col_send,
    col_recv,
    row_send,
    row_recv,
    made_send,
    relay_send,
    near_recv,
    stat_send,
    stat_recv,
):
    me = lax.axis_index("tm")
    count, width = tokens_ref.shape
    row_tokens = count // n
    pair_tokens = 2 * row_tokens
    chunks = count // CHUNK
    share = n // (2 * chunks)
    head_dim = width // HEADS
    channels = gain_ref.shape[1]
    blocks = width // BLOCK
    heads_per = BLOCK // head_dim
    group_size = channels // NORM_GROUPS

    levels = n // 4
    level = lax.div(me, 4)
    y = lax.rem(lax.div(me, 2), 2)
    core = lax.rem(me, 2)
    side = lax.div(me, n // 2)
    place = lax.div(me, n // chunks)
    inward = place + side * (chunks - 1 - 2 * place)
    inner = inward == 1
    mine = 2 * level + core
    core_peer = me + 1 - 2 * core
    row_peer = me + 2 - 4 * y

    def facing(k):
        return k + side * (chunks - 1 - 2 * k)

    def frame_of(source, column):
        return 4 * lax.div(source, 2) + 2 * column + lax.rem(source, 2)

    loads = [
        pltpu.make_async_copy(a, b, load_sem.at[i])
        for i, (a, b) in enumerate(
            [
                (tokens_hbm, tokens_ref),
                (qkv_hbm, qkv_ref),
                (out_hbm, outw_ref),
                (conv_hbm, convw_ref),
            ]
        )
    ]
    for load in loads:
        load.start()

    barrier = pltpu.get_barrier_semaphore()

    @pl.loop(1, n)
    def _(s):
        pl.semaphore_signal(
            barrier, inc=1, device_id={"tm": lax.rem(me + s, n)}, device_id_type=MESH
        )

    def remote(src, dst, send_sem, recv_sem, device):
        return pltpu.make_async_remote_copy(
            src_ref=src,
            dst_ref=dst,
            send_sem=send_sem,
            recv_sem=recv_sem,
            device_id={"tm": device},
            device_id_type=MESH,
        )

    def tok_copy(slot):
        return remote(
            sent_tokens.at[slot],
            tile_tokens.at[mine],
            tok_send.at[slot],
            tok_recv.at[mine],
            4 * lax.div(slot, 2) + 2 * y + lax.rem(slot, 2),
        )

    def tok_arrival(source):
        return remote(
            sent_tokens.at[source],
            tile_tokens.at[source],
            tok_send.at[source],
            tok_recv.at[source],
            4 * lax.div(source, 2) + 2 * y + lax.rem(source, 2),
        )

    def column_copy(k):
        return remote(
            sent_state,
            all_state.at[me],
            col_send.at[k],
            col_recv.at[k],
            lax.rem(me + 4 * k, n),
        )

    def pass_on(source, peer, send_sem, recv_sem):
        return remote(all_state.at[source], all_state.at[source], send_sem, recv_sem, peer)

    def row_pass(k):
        source = lax.rem(me + n - 4 * k, n)
        return pass_on(source, row_peer, row_send.at[k], row_recv.at[k])

    def core_pass(k, d):
        source = lax.rem(me + d * (row_peer - me) + n - 4 * k, n)
        return pass_on(source, core_peer, core_send.at[d, k], core_recv.at[d, k])

    def stat_copy(s):
        return remote(
            sent_stat,
            all_stat.at[me],
            stat_send.at[s],
            stat_recv.at[s],
            lax.rem(me + s, n),
        )

    across = lax.rem(y + core, 2)
    outer_owner = 4 * level + 3 * core
    inner_owner = 4 * level + 1 + core
    beyond = 4 * level - 1 + 5 * core
    exists = jnp.logical_and(beyond >= 0, beyond < n)
    beyond_device = jnp.clip(beyond, 0, n - 1)
    far_slot = 2 * core
    peer_slot = 2 - 2 * core

    def made_copy(kind, c):
        if kind == 0:
            part, device, slot = 1 - core, inner_owner, 1
        elif kind == 1:
            part, device, slot = core, beyond_device, peer_slot
        elif kind == 2:
            part = core
            device = across * outer_owner + (1 - across) * inner_owner
            slot = across + (1 - across) * far_slot
        else:
            part, device, slot = 1 - core, 4 * level + 2 - core, far_slot
        return remote(
            made.at[part, c],
            near_rows.at[slot, c, y],
            made_send.at[kind, c],
            near_recv.at[slot, c, y],
            device,
        )

    def relay_copy(c):
        return remote(
            near_rows.at[1, c, 1 - y],
            near_rows.at[far_slot, c, 1 - y],
            relay_send.at[c],
            near_recv.at[far_slot, c, 1 - y],
            core_peer,
        )

    def near_arrival(slot, c, column):
        return remote(
            near_rows.at[slot, c, column],
            near_rows.at[slot, c, column],
            made_send.at[0, c],
            near_recv.at[slot, c, column],
            core_peer,
        )

    loads[0].wait()

    def permute(to):
        where = lax.broadcasted_iota(jnp.int32, (CHUNK, count), 0) + to * CHUNK
        pick = jnp.where(order_ref[...] == where, 1.0, 0.0).astype(BF16)
        moved = jnp.dot(pick, tokens_ref[...], preferred_element_type=F32)
        sent_tokens[pl.ds(to * share, share)] = moved.reshape(share, pair_tokens, width).astype(
            BF16
        )

    def send_tiles(to):
        @pl.loop(0, share)
        def _(k):
            slot = to * share + k

            @pl.when(slot != mine)
            def _():
                tok_copy(slot).start()

    targets = [facing(x) for x in (inward + 1, inward * 0, 2 - inward, inward * 0 + 3)]

    loads[1].wait()
    state_acc[...] = jnp.zeros_like(state_acc)
    sum_acc[...] = jnp.zeros_like(sum_acc)

    @pl.loop(0, chunks)
    def _(c):
        rows = pl.ds(pl.multiple_of(c * CHUNK, CHUNK), CHUNK)
        mixed = jnp.dot(
            tokens_ref[rows, :], qkv_ref[:, width : 3 * width], preferred_element_type=F32
        ).astype(BF16)
        keys = jnp.maximum(mixed[:, :width], jnp.zeros((), BF16))
        sum_acc[...] += keys.astype(F32).reshape(CHUNK // 8, 8, width).sum(axis=0)
        for b in range(blocks):
            lanes = slice(b * BLOCK, (b + 1) * BLOCK)
            state_acc[b] += lax.dot_general(
                keys[:, lanes],
                mixed[:, width + b * BLOCK : width + (b + 1) * BLOCK],
                (((0,), (0,)), ((), ())),
                preferred_element_type=F32,
            )

    head_row = lax.broadcasted_iota(jnp.int32, (BLOCK, BLOCK), 0) // head_dim
    head_col = lax.broadcasted_iota(jnp.int32, (BLOCK, BLOCK), 1) // head_dim
    same_head = head_row == head_col
    pieces = width // 128
    sum_at = pieces * head_dim
    for b in range(blocks):
        own = jnp.where(same_head, state_acc[b], 0.0)
        own = own.reshape(heads_per, head_dim, BLOCK).sum(axis=0).astype(BF16)
        for i in range(BLOCK // 128):
            at = (b * (BLOCK // 128) + i) * head_dim
            sent_state[at : at + head_dim, :] = own[:, i * 128 : (i + 1) * 128]
    key_sum = jnp.sum(sum_acc[...], axis=0, keepdims=True)
    high = key_sum.astype(BF16).astype(F32)
    line = lax.broadcasted_iota(jnp.int32, (16, 128), 0)
    packed = jnp.zeros((16, 128), F32)
    for i in range(pieces):
        lanes = slice(i * 128, (i + 1) * 128)
        packed = jnp.where(line == i, high[:, lanes], packed)
        packed = jnp.where(line == pieces + i, (key_sum - high)[:, lanes], packed)
    sent_state[sum_at : sum_at + 16, :] = packed.astype(BF16)

    all_state[me] = sent_state[...]

    pl.semaphore_wait(barrier, n - 1)

    @pl.loop(1, levels)
    def _(k):
        column_copy(k).start()

    row_pass(0).start()
    core_pass(0, 0).start()

    permute(targets[0])
    send_tiles(targets[0])
    permute(targets[1])
    send_tiles(targets[1])

    @pl.loop(0, chunks // 2)
    def _(k):
        permute(facing((1 - k) * (2 - inward) + k * 3))

    tile_tokens[mine] = sent_tokens[mine]

    send_tiles(targets[2])
    send_tiles(targets[3])

    @pl.loop(1, levels)
    def _(k):
        column_copy(k).wait_recv()
        row_pass(k).start()
        core_pass(k, 0).start()

    @pl.loop(0, levels)
    def _(k):
        row_pass(k).wait_recv()
        core_pass(k, 1).start()

    def attend_order(k):
        late = lax.div(k, 2)
        return facing(
            (1 - late) * (inward + k * (1 - 2 * inward))
            + late * ((3 - k) * (3 - inward) + (k - 2) * (2 + inward))
        )

    def queries(c):
        @pl.loop(0, share)
        def _(k):
            source = c * share + k

            @pl.when(source != mine)
            def _():
                tok_arrival(source).wait_recv()

        mixed = jnp.dot(
            flat(tile_tokens[pl.ds(c * share, share)]),
            qkv_ref[:, 0:width],
            preferred_element_type=F32,
        ).astype(BF16)
        rows = pl.ds(pl.multiple_of(c * CHUNK, CHUNK), CHUNK)
        rows_ref[rows, :] = jnp.maximum(mixed, jnp.zeros((), BF16)).astype(F32)

    queries(attend_order(0))

    @pl.loop(0, levels)
    def _(k):
        core_pass(k, 0).wait_recv()
        core_pass(k, 1).wait_recv()

    running[...] = jnp.zeros_like(running)
    prefix[...] = jnp.zeros_like(prefix)

    @pl.loop(0, n)
    def _(f):
        new_group = group_ref[f] != group_ref[jnp.maximum(f - 1, 0)]
        before = jnp.where(new_group, running[...], prefix[...])
        prefix[...] = before
        own = all_state[f].astype(F32)
        running[...] += own
        all_total[f] = before + own

    head_ones = same_head.astype(F32).astype(BF16)
    reach = 3 * channels

    def attend_chunk(c):
        rows = pl.ds(pl.multiple_of(c * CHUNK, CHUNK), CHUNK)

        def attend(k, carry):
            total = all_total[frame_of(c * share + k, y)]
            key_total = jnp.concatenate(
                [
                    total[sum_at + i : sum_at + i + 1, :]
                    + total[sum_at + pieces + i : sum_at + pieces + i + 1, :]
                    for i in range(pieces)
                ],
                axis=1,
            )
            here = pl.ds(pl.multiple_of(c * CHUNK + k * pair_tokens, 16), pair_tokens)
            query = rows_ref[here, :]
            scaled = (query * key_total).astype(BF16)
            query = query.astype(BF16)
            for b in range(blocks):
                lanes = slice(b * BLOCK, (b + 1) * BLOCK)
                first = b * (BLOCK // 128)
                state = jnp.concatenate(
                    [
                        total[i * head_dim : (i + 1) * head_dim, :]
                        for i in range(first, first + BLOCK // 128)
                    ],
                    axis=1,
                )
                high = state.astype(BF16).astype(F32)
                numer = jnp.zeros((pair_tokens, BLOCK), F32)
                for part in (high, state - high):
                    spread = jnp.concatenate([part] * heads_per, axis=0)
                    spread = jnp.where(same_head, spread, 0.0).astype(BF16)
                    numer += jnp.dot(query[:, lanes], spread, preferred_element_type=F32)
                denom = jnp.dot(scaled[:, lanes], head_ones, preferred_element_type=F32) + 1.0
                rows_ref[here, lanes] = numer / denom
            return carry

        lax.fori_loop(0, share, attend, 0, unroll=share <= 4)
        attended = rows_ref[rows, :].reshape(share, 2, row_tokens, width)
        for i in range(2):
            made[i, c] = attended[:, i].astype(BF16)
        made_copy(0, c).start()
        made_copy(2, c).start()

        @pl.when(across == 0)
        def _():
            made_copy(3, c).start()

        @pl.when(across == 0)
        def _():
            near_rows[1, c, y] = made[core, c]
            near_rows[peer_slot, c, y] = made[1 - core, c]

        @pl.when(across == 1)
        def _():
            near_rows[far_slot, c, y] = made[1 - core, c]

    attend_chunk(attend_order(0))
    queries(attend_order(1))
    attend_chunk(attend_order(1))

    loads[2].wait()
    loads[3].wait()

    def widen(even, odd):
        column = lax.rem(lax.broadcasted_iota(jnp.int32, even.shape, 0), row_tokens)
        odd_left = jnp.where(column == 0, 0.0, pltpu.roll(odd, 1, 0))
        even_right = jnp.where(column == row_tokens - 1, 0.0, pltpu.roll(even, CHUNK - 1, 0))
        return [x.astype(BF16) for x in (odd_left, even, odd, even_right)]

    valid = valid_ref[me]
    valid_above = jnp.where(me > 0, valid_ref[jnp.maximum(me - 1, 0)], 0)
    valid_below = jnp.where(me < n - 1, valid_ref[jnp.minimum(me + 1, n - 1)], 0)
    valid_rows = valid * row_tokens

    outer = across == 0
    half = 2 * channels
    limits = (valid_above, valid, valid, valid_below)

    def frames_here():
        row = lax.broadcasted_iota(jnp.int32, (CHUNK, channels), 0)
        step = lax.div(row, row_tokens)
        return lax.rem(step, share), lax.div(step, share)

    def chunk_frames(c):
        k, column = frames_here()
        return frame_of(c * share + k, column)

    def place_line(p, line, frame, limit):
        live = frame < limit
        even = jnp.where(live, line[:, :channels], 0.0)
        odd = jnp.where(live, line[:, channels:], 0.0)
        for i, part in enumerate(widen(even, odd)):
            cells[p, :, i * channels : (i + 1) * channels] = part

    def out_pixels(c, b):
        return pl.ds(c * 2 * CHUNK + b, CHUNK, 2)

    def gather_stats(c, r, results, live):
        eights = [x.reshape(CHUNK // 8, 8, channels).sum(axis=0) for x in results]
        total = jnp.sum(eights[0] + eights[1], axis=0, keepdims=True)
        size = jnp.clip(valid_rows - c * CHUNK, 0, CHUNK) * 2
        centre = total / jnp.maximum(size, 1).astype(F32)
        square = jnp.zeros((8, channels), F32)
        for x in results:
            off = jnp.where(live, x - centre, 0.0)
            square += (off * off).reshape(CHUNK // 8, 8, channels).sum(axis=0)
        square = jnp.sum(square, axis=0, keepdims=True)
        line = lax.broadcasted_iota(jnp.int32, (8, channels), 0)
        stat_acc[2 * c + r] = jnp.where(
            line == 0, total, jnp.where(line == 1, square, size.astype(F32))
        )

    def relay(c):
        near_arrival(1, c, 1 - y).wait_recv()
        relay_copy(c).start()

    def decode(c, defer):
        @pl.when(jnp.logical_not(outer))
        def _():
            near_arrival(1, c, y).wait_recv()
            near_arrival(peer_slot, c, y).wait_recv()
            near_arrival(far_slot, c, 1 - y).wait_recv()

        if not defer:

            @pl.when(jnp.logical_and(outer, exists))
            def _():
                near_arrival(far_slot, c, y).wait_recv()
                near_arrival(far_slot, c, 1 - y).wait_recv()

        frame = chunk_frames(c)
        own = jnp.dot(flat(near_rows[1, c]), outw_ref[...], preferred_element_type=F32)
        place_line(1, own[:, :half], frame, valid)
        place_line(2, own[:, half:], frame, valid)
        near_arrival(peer_slot, c, 1 - y).wait_recv()
        absent = outer if defer else jnp.logical_and(outer, jnp.logical_not(exists))
        for p, slot, low in ((0, 0, half), (3, 2, 0)):
            missing = jnp.logical_and(absent, far_slot == slot)

            @pl.when(missing)
            def _():
                cells[p] = jnp.zeros(cells.shape[1:], BF16)

            @pl.when(jnp.logical_not(missing))
            def _():
                line = jnp.dot(
                    flat(near_rows[slot, c]),
                    outw_ref[:, low : low + half],
                    preferred_element_type=F32,
                )
                place_line(p, line, frame, limits[p])

        live = frame < valid
        for r in range(2):
            results = []
            for b in range(2):
                lanes = slice(b * channels, b * channels + reach)
                result = sum(
                    jnp.dot(cells[r + d, :, lanes], convw_ref[d], preferred_element_type=F32)
                    for d in range(3)
                )
                result = jnp.where(live, result, 0.0)
                results.append(result)
                for h in range(0, channels, 128):
                    out_buf[r, h // 128, out_pixels(c, b), :] = result[:, h : h + 128]
            gather_stats(c, r, results, live)

    def finish(c):
        near_arrival(far_slot, c, y).wait_recv()
        near_arrival(far_slot, c, 1 - y).wait_recv()
        frame = chunk_frames(c)
        line = jnp.dot(
            flat(near_rows[far_slot, c]),
            outw_ref[:, pl.ds(pl.multiple_of((1 - core) * half, half), half)],
            preferred_element_type=F32,
        )
        place_line(0, line, frame, jnp.where(core == 0, valid_above, valid_below))
        live = frame < valid
        results = []
        for b in range(2):
            lanes = slice(b * channels, b * channels + reach)
            result = jnp.dot(cells[0, :, lanes], convw_ref[far_slot], preferred_element_type=F32)
            before = jnp.concatenate(
                [out_buf[core, h, out_pixels(c, b), :] for h in range(channels // 128)], axis=1
            )
            result = before + jnp.where(live, result, 0.0)
            results.append(result)
            for h in range(0, channels, 128):
                out_buf[core, h // 128, out_pixels(c, b), :] = result[:, h : h + 128]
        gather_stats(c, core, results, live)

    def reach_beyond(*steps):
        @pl.when(exists)
        def _():
            for k in steps:
                made_copy(1, attend_order(k)).start()

    def first_decode():
        decode(attend_order(0), True)

    @pl.when(jnp.logical_and(inner, core == 1))
    def _():
        reach_beyond(0, 1)
        relay(attend_order(0))
        first_decode()

    @pl.when(jnp.logical_not(inner))
    def _():
        relay(attend_order(0))

    queries(attend_order(2))
    attend_chunk(attend_order(2))

    @pl.when(jnp.logical_not(jnp.logical_and(inner, core == 1)))
    def _():
        reach_beyond(0, 1)

    @pl.when(jnp.logical_not(inner))
    def _():
        first_decode()

    queries(attend_order(3))
    attend_chunk(attend_order(3))
    reach_beyond(2, 3)

    @pl.when(jnp.logical_and(inner, core == 0))
    def _():
        relay(attend_order(0))
        first_decode()

    relay(attend_order(1))

    decode(attend_order(1), True)
    relay(attend_order(2))
    decode(attend_order(2), True)

    @pl.when(jnp.logical_and(outer, exists))
    def _():
        @pl.loop(0, 2)
        def _(k):
            finish(attend_order(k))

    relay(attend_order(3))

    @pl.when(jnp.logical_and(outer, exists))
    def _():
        finish(attend_order(2))

    decode(attend_order(3), False)

    group_row = lax.broadcasted_iota(jnp.int32, (channels, channels), 0) // group_size
    group_col = lax.broadcasted_iota(jnp.int32, (channels, channels), 1) // group_size
    group_ones = jnp.where(group_row == group_col, 1.0, 0.0).astype(BF16)

    def group_total(sums):
        parts = []
        for _ in range(3):
            part = sums.astype(BF16)
            parts.append(part)
            sums = sums - part.astype(F32)
        line = lax.broadcasted_iota(jnp.int32, (16, channels), 0)
        stacked = jnp.zeros((16, channels), F32)
        for i, part in enumerate(parts):
            stacked = jnp.where(line == i, part.astype(F32), stacked)
        found = jnp.dot(stacked.astype(BF16), group_ones, preferred_element_type=F32)
        return found[0:1] + found[1:2] + found[2:3]

    def combine(total, square, size):
        whole = jnp.sum(size, axis=0, keepdims=True)
        mean = jnp.sum(total, axis=0, keepdims=True) / whole
        off = total / jnp.maximum(size, 1.0) - mean
        return mean, jnp.sum(square + size * (off * off), axis=0, keepdims=True), whole

    mean, square, whole = combine(*[stat_acc[:, i, :] for i in range(3)])
    halves = channels // 128
    line = lax.broadcasted_iota(jnp.int32, (8, 128), 0)
    packed = jnp.zeros((8, 128), F32)
    for i, field in enumerate((mean * whole, square, whole)):
        for h in range(halves):
            packed = jnp.where(line == i * halves + h, field[:, h * 128 : (h + 1) * 128], packed)
    sent_stat[...] = packed

    @pl.loop(1, n)
    def _(s):
        stat_copy(s + (1 - side) * (n - 2 * s)).start()

    all_stat[me] = sent_stat[...]

    @pl.loop(0, n // 2)
    def _(slot):
        @pl.when(slot != mine)
        def _():
            tok_copy(slot).wait_send()

    @pl.loop(0, chunks)
    def _(c):
        made_copy(0, c).wait_send()
        made_copy(2, c).wait_send()
        relay_copy(c).wait_send()

        @pl.when(across == 0)
        def _():
            made_copy(3, c).wait_send()

        @pl.when(exists)
        def _():
            made_copy(1, c).wait_send()

    @pl.loop(1, levels)
    def _(k):
        column_copy(k).wait_send()

    @pl.loop(0, levels)
    def _(k):
        row_pass(k).wait_send()
        core_pass(k, 0).wait_send()
        core_pass(k, 1).wait_send()

    @pl.loop(1, n)
    def _(s):
        stat_copy(s).wait_recv()

    mean, square, whole = combine(
        *[
            jnp.concatenate([all_stat[:, i * halves + h, :] for h in range(halves)], axis=1)
            for i in range(3)
        ]
    )
    group_mean = group_total(mean) / group_size
    off = mean - group_mean
    group_square = group_total(square + whole * (off * off))
    mean = group_mean
    scale = gain_ref[...] * lax.rsqrt(group_square / (whole * group_size) + 1e-05)
    sides = [(r, h) for r in range(2) for h in range(channels // 128)]
    half_scale = 0.5 * scale
    half_shift = 0.5 * (bias_ref[...] - mean * scale)

    @pl.loop(0, n)
    def _(s):
        pixels = pl.ds(pl.multiple_of(s * 2 * row_tokens, 8), 2 * row_tokens)
        step = lax.rem(s, 2 * share)
        f = frame_of(lax.div(s, 2 * share) * share + lax.rem(step, share), lax.div(step, share))
        live = f < valid
        for r, h in sides:
            lanes = slice(h * 128, (h + 1) * 128)
            normed = out_buf[r, h, pixels, :] * half_scale[:, lanes] + half_shift[:, lanes]
            silu = normed + normed * jnp.tanh(normed)
            decoded_ref[f, r, :, lanes] = jnp.where(live, silu, 0.0).astype(BF16)

    @pl.loop(1, n)
    def _(s):
        stat_copy(s).wait_send()


def local(
    tokens,
    qkv_weight,
    out_weight,
    conv_weight,
    norm_gain,
    norm_bias,
    group_map,
    token_order,
    valid_frames,
):
    n = lax.axis_size("tm")
    count, width = tokens.shape
    channels = conv_weight.shape[3]
    row_tokens = count // n
    chunks = count // CHUNK
    share = n // (2 * chunks)
    state_shape = (width // 128 * (width // HEADS) + 16, 128)
    anywhere = pl.BlockSpec(memory_space=pltpu.HBM)
    vmem = pl.BlockSpec(memory_space=pltpu.VMEM)
    smem = pl.BlockSpec(memory_space=pltpu.SMEM)
    dma = pltpu.SemaphoreType.DMA
    return pl.pallas_call(
        functools.partial(mega, n),
        out_shape=pltpu.VMEM((n, 2, 2 * row_tokens, channels), BF16),
        in_specs=[anywhere] * 4 + [vmem, vmem, smem, vmem, smem],
        out_specs=vmem,
        scratch_shapes=[
            pltpu.VMEM((count, width), BF16),
            pltpu.VMEM((width, 3 * width), BF16),
            pltpu.VMEM((width, 4 * channels), BF16),
            pltpu.VMEM((3, 3 * channels, channels), BF16),
            pltpu.VMEM((n // 2, 2 * row_tokens, width), BF16),
            pltpu.VMEM((n // 2, 2 * row_tokens, width), BF16),
            pltpu.VMEM((width // BLOCK, BLOCK, BLOCK), F32),
            pltpu.VMEM((8, width), F32),
            pltpu.VMEM(state_shape, BF16),
            pltpu.VMEM((n,) + state_shape, BF16),
            pltpu.VMEM((n,) + state_shape, F32),
            pltpu.VMEM(state_shape, F32),
            pltpu.VMEM(state_shape, F32),
            pltpu.VMEM((count, width), F32),
            pltpu.VMEM((2, chunks, share, row_tokens, width), BF16),
            pltpu.VMEM((3, chunks, 2, share, row_tokens, width), BF16),
            pltpu.VMEM((4, CHUNK, 4 * channels), BF16),
            pltpu.VMEM((2 * chunks, 8, channels), F32),
            pltpu.VMEM((8, 128), F32),
            pltpu.VMEM((n, 8, 128), F32),
            pltpu.VMEM((2, channels // 128, 2 * count, 128), F32),
            dma((4,)),
            dma((n // 2,)),
            dma((n // 2,)),
            dma((2, n // 4)),
            dma((2, n // 4)),
            dma((n // 4,)),
            dma((n // 4,)),
            dma((n // 4,)),
            dma((n // 4,)),
            dma((4, chunks)),
            dma((chunks,)),
            dma((3, chunks, 2)),
            dma((n,)),
            dma((n,)),
        ],
        compiler_params=pltpu.CompilerParams(
            collective_id=0, has_side_effects=True, vmem_limit_bytes=VMEM - 2 * count * 4 * channels
        ),
    )(
        tokens,
        qkv_weight,
        out_weight,
        conv_weight.reshape(3, 3 * channels, channels),
        norm_gain[None],
        norm_bias[None],
        group_map,
        token_order[None],
        valid_frames,
    )


def solution(mesh):
    in_specs = (P(("clip", "tm"), None), P(), P(), P(), P(), P(), P("clip"), P("clip"), P("clip"))
    out_specs = P("clip", "tm", None, None)
    return jax.shard_map(local, mesh=mesh, in_specs=in_specs, out_specs=out_specs, check_vma=False)
```

```python
import functools

import jax
import jax.numpy as jnp
from jax import lax
from jax.experimental import pallas as pl
from jax.experimental.pallas import tpu as pltpu
from jax.sharding import PartitionSpec as P

HEADS = 16
NORM_GROUPS = 32
MESH = pl.DeviceIdType.MESH
F32 = jnp.float32
BF16 = jnp.bfloat16
CHUNK = 256
BLOCK = 256
VMEM = 66650112


def flat(cells):
    rows, width = cells.shape[-2:]
    every = cells.size // width
    if rows % 16 == 0:
        return cells.reshape(every, width)
    return cells.astype(F32).reshape(every, width).astype(BF16)


def mega(
    n,
    tokens_hbm,
    qkv_hbm,
    out_hbm,
    conv_hbm,
    gain_ref,
    bias_ref,
    group_ref,
    order_ref,
    valid_ref,
    decoded_ref,
    tokens_ref,
    qkv_ref,
    outw_ref,
    convw_ref,
    sent_tokens,
    tile_tokens,
    state_acc,
    sum_acc,
    sent_state,
    all_state,
    all_total,
    running,
    prefix,
    rows_ref,
    made,
    near_rows,
    cells,
    stat_acc,
    sent_stat,
    all_stat,
    out_buf,
    load_sem,
    tok_send,
    tok_recv,
    core_send,
    core_recv,
    col_send,
    col_recv,
    row_send,
    row_recv,
    made_send,
    relay_send,
    near_recv,
    stat_send,
    stat_recv,
):
    me = lax.axis_index("tm")
    count, width = tokens_ref.shape
    row_tokens = count // n
    pair_tokens = 2 * row_tokens
    chunks = count // CHUNK
    share = n // (2 * chunks)
    head_dim = width // HEADS
    channels = gain_ref.shape[1]
    blocks = width // BLOCK
    heads_per = BLOCK // head_dim
    group_size = channels // NORM_GROUPS

    levels = n // 4
    level = lax.div(me, 4)
    y = lax.rem(lax.div(me, 2), 2)
    core = lax.rem(me, 2)
    side = lax.div(me, n // 2)
    place = lax.div(me, n // chunks)
    inward = place + side * (chunks - 1 - 2 * place)
    inner = inward == 1
    mine = 2 * level + core
    core_peer = me + 1 - 2 * core
    row_peer = me + 2 - 4 * y

    def facing(k):
        return k + side * (chunks - 1 - 2 * k)

    def frame_of(source, column):
        return 4 * lax.div(source, 2) + 2 * column + lax.rem(source, 2)

    loads = [
        pltpu.make_async_copy(a, b, load_sem.at[i])
        for i, (a, b) in enumerate(
            [
                (tokens_hbm, tokens_ref),
                (qkv_hbm, qkv_ref),
                (out_hbm, outw_ref),
                (conv_hbm, convw_ref),
            ]
        )
    ]
    for load in loads:
        load.start()

    barrier = pltpu.get_barrier_semaphore()

    @pl.loop(1, n)
    def _(s):
        pl.semaphore_signal(
            barrier, inc=1, device_id={"tm": lax.rem(me + s, n)}, device_id_type=MESH
        )

    def remote(src, dst, send_sem, recv_sem, device):
        return pltpu.make_async_remote_copy(
            src_ref=src,
            dst_ref=dst,
            send_sem=send_sem,
            recv_sem=recv_sem,
            device_id={"tm": device},
            device_id_type=MESH,
        )

    def tok_copy(slot):
        return remote(
            sent_tokens.at[slot],
            tile_tokens.at[mine],
            tok_send.at[slot],
            tok_recv.at[mine],
            4 * lax.div(slot, 2) + 2 * y + lax.rem(slot, 2),
        )

    def tok_arrival(source):
        return remote(
            sent_tokens.at[source],
            tile_tokens.at[source],
            tok_send.at[source],
            tok_recv.at[source],
            4 * lax.div(source, 2) + 2 * y + lax.rem(source, 2),
        )

    def column_copy(k):
        return remote(
            sent_state,
            all_state.at[me],
            col_send.at[k],
            col_recv.at[k],
            lax.rem(me + 4 * k, n),
        )

    def pass_on(source, peer, send_sem, recv_sem):
        return remote(all_state.at[source], all_state.at[source], send_sem, recv_sem, peer)

    def row_pass(k):
        source = lax.rem(me + n - 4 * k, n)
        return pass_on(source, row_peer, row_send.at[k], row_recv.at[k])

    def core_pass(k, d):
        source = lax.rem(me + d * (row_peer - me) + n - 4 * k, n)
        return pass_on(source, core_peer, core_send.at[d, k], core_recv.at[d, k])

    def stat_copy(s):
        return remote(
            sent_stat,
            all_stat.at[me],
            stat_send.at[s],
            stat_recv.at[s],
            lax.rem(me + s, n),
        )

    across = lax.rem(y + core, 2)
    outer_owner = 4 * level + 3 * core
    inner_owner = 4 * level + 1 + core
    beyond = 4 * level - 1 + 5 * core
    exists = jnp.logical_and(beyond >= 0, beyond < n)
    beyond_device = jnp.clip(beyond, 0, n - 1)
    far_slot = 2 * core
    peer_slot = 2 - 2 * core

    def made_copy(kind, c):
        if kind == 0:
            part, device, slot = 1 - core, inner_owner, 1
        elif kind == 1:
            part, device, slot = core, beyond_device, peer_slot
        elif kind == 2:
            part = core
            device = across * outer_owner + (1 - across) * inner_owner
            slot = across + (1 - across) * far_slot
        else:
            part, device, slot = 1 - core, 4 * level + 2 - core, far_slot
        return remote(
            made.at[part, c],
            near_rows.at[slot, c, y],
            made_send.at[kind, c],
            near_recv.at[slot, c, y],
            device,
        )

    def relay_copy(c):
        return remote(
            near_rows.at[1, c, 1 - y],
            near_rows.at[far_slot, c, 1 - y],
            relay_send.at[c],
            near_recv.at[far_slot, c, 1 - y],
            core_peer,
        )

    def near_arrival(slot, c, column):
        return remote(
            near_rows.at[slot, c, column],
            near_rows.at[slot, c, column],
            made_send.at[0, c],
            near_recv.at[slot, c, column],
            core_peer,
        )

    loads[0].wait()

    def permute(to):
        where = lax.broadcasted_iota(jnp.int32, (CHUNK, count), 0) + to * CHUNK
        pick = jnp.where(order_ref[...] == where, 1.0, 0.0).astype(BF16)
        moved = jnp.dot(pick, tokens_ref[...], preferred_element_type=F32)
        sent_tokens[pl.ds(to * share, share)] = moved.reshape(share, pair_tokens, width).astype(
            BF16
        )

    def send_tiles(to):
        @pl.loop(0, share)
        def _(k):
            slot = to * share + k

            @pl.when(slot != mine)
            def _():
                tok_copy(slot).start()

    targets = [facing(x) for x in (inward + 1, inward * 0, 2 - inward, inward * 0 + 3)]

    loads[1].wait()
    state_acc[...] = jnp.zeros_like(state_acc)
    sum_acc[...] = jnp.zeros_like(sum_acc)

    @pl.loop(0, chunks)
    def _(c):
        rows = pl.ds(pl.multiple_of(c * CHUNK, CHUNK), CHUNK)
        mixed = jnp.dot(
            tokens_ref[rows, :], qkv_ref[:, width : 3 * width], preferred_element_type=F32
        ).astype(BF16)
        keys = jnp.maximum(mixed[:, :width], jnp.zeros((), BF16))
        sum_acc[...] += keys.astype(F32).reshape(CHUNK // 8, 8, width).sum(axis=0)
        for b in range(blocks):
            lanes = slice(b * BLOCK, (b + 1) * BLOCK)
            state_acc[b] += lax.dot_general(
                keys[:, lanes],
                mixed[:, width + b * BLOCK : width + (b + 1) * BLOCK],
                (((0,), (0,)), ((), ())),
                preferred_element_type=F32,
            )

    head_row = lax.broadcasted_iota(jnp.int32, (BLOCK, BLOCK), 0) // head_dim
    head_col = lax.broadcasted_iota(jnp.int32, (BLOCK, BLOCK), 1) // head_dim
    same_head = head_row == head_col
    pieces = width // 128
    sum_at = pieces * head_dim
    for b in range(blocks):
        own = jnp.where(same_head, state_acc[b], 0.0)
        own = own.reshape(heads_per, head_dim, BLOCK).sum(axis=0).astype(BF16)
        for i in range(BLOCK // 128):
            at = (b * (BLOCK // 128) + i) * head_dim
            sent_state[at : at + head_dim, :] = own[:, i * 128 : (i + 1) * 128]
    key_sum = jnp.sum(sum_acc[...], axis=0, keepdims=True)
    high = key_sum.astype(BF16).astype(F32)
    line = lax.broadcasted_iota(jnp.int32, (16, 128), 0)
    packed = jnp.zeros((16, 128), F32)
    for i in range(pieces):
        lanes = slice(i * 128, (i + 1) * 128)
        packed = jnp.where(line == i, high[:, lanes], packed)
        packed = jnp.where(line == pieces + i, (key_sum - high)[:, lanes], packed)
    sent_state[sum_at : sum_at + 16, :] = packed.astype(BF16)

    all_state[me] = sent_state[...]

    pl.semaphore_wait(barrier, n - 1)

    @pl.loop(1, levels)
    def _(k):
        column_copy(k).start()

    row_pass(0).start()
    core_pass(0, 0).start()

    permute(targets[0])
    send_tiles(targets[0])
    permute(targets[1])
    send_tiles(targets[1])

    @pl.loop(0, chunks // 2)
    def _(k):
        permute(facing((1 - k) * (2 - inward) + k * 3))

    tile_tokens[mine] = sent_tokens[mine]

    send_tiles(targets[2])
    send_tiles(targets[3])

    @pl.loop(1, levels)
    def _(k):
        column_copy(k).wait_recv()
        row_pass(k).start()
        core_pass(k, 0).start()

    @pl.loop(0, levels)
    def _(k):
        row_pass(k).wait_recv()
        core_pass(k, 1).start()

    def attend_order(k):
        late = lax.div(k, 2)
        return facing(
            (1 - late) * (inward + k * (1 - 2 * inward))
            + late * ((3 - k) * (3 - inward) + (k - 2) * (2 + inward))
        )

    def queries(c):
        @pl.loop(0, share)
        def _(k):
            source = c * share + k

            @pl.when(source != mine)
            def _():
                tok_arrival(source).wait_recv()

        mixed = jnp.dot(
            flat(tile_tokens[pl.ds(c * share, share)]),
            qkv_ref[:, 0:width],
            preferred_element_type=F32,
        ).astype(BF16)
        rows = pl.ds(pl.multiple_of(c * CHUNK, CHUNK), CHUNK)
        rows_ref[rows, :] = jnp.maximum(mixed, jnp.zeros((), BF16)).astype(F32)

    queries(attend_order(0))

    @pl.loop(0, levels)
    def _(k):
        core_pass(k, 0).wait_recv()
        core_pass(k, 1).wait_recv()

    running[...] = jnp.zeros_like(running)
    prefix[...] = jnp.zeros_like(prefix)

    @pl.loop(0, n)
    def _(f):
        new_group = group_ref[f] != group_ref[jnp.maximum(f - 1, 0)]
        before = jnp.where(new_group, running[...], prefix[...])
        prefix[...] = before
        own = all_state[f].astype(F32)
        running[...] += own
        all_total[f] = before + own

    head_ones = same_head.astype(F32).astype(BF16)
    reach = 3 * channels

    def attend_chunk(c):
        rows = pl.ds(pl.multiple_of(c * CHUNK, CHUNK), CHUNK)

        def attend(k, carry):
            total = all_total[frame_of(c * share + k, y)]
            key_total = jnp.concatenate(
                [
                    total[sum_at + i : sum_at + i + 1, :]
                    + total[sum_at + pieces + i : sum_at + pieces + i + 1, :]
                    for i in range(pieces)
                ],
                axis=1,
            )
            here = pl.ds(pl.multiple_of(c * CHUNK + k * pair_tokens, 16), pair_tokens)
            query = rows_ref[here, :]
            scaled = (query * key_total).astype(BF16)
            query = query.astype(BF16)
            for b in range(blocks):
                lanes = slice(b * BLOCK, (b + 1) * BLOCK)
                first = b * (BLOCK // 128)
                state = jnp.concatenate(
                    [
                        total[i * head_dim : (i + 1) * head_dim, :]
                        for i in range(first, first + BLOCK // 128)
                    ],
                    axis=1,
                )
                high = state.astype(BF16).astype(F32)
                numer = jnp.zeros((pair_tokens, BLOCK), F32)
                for part in (high, state - high):
                    spread = jnp.concatenate([part] * heads_per, axis=0)
                    spread = jnp.where(same_head, spread, 0.0).astype(BF16)
                    numer += jnp.dot(query[:, lanes], spread, preferred_element_type=F32)
                denom = jnp.dot(scaled[:, lanes], head_ones, preferred_element_type=F32) + 1.0
                rows_ref[here, lanes] = numer / denom
            return carry

        lax.fori_loop(0, share, attend, 0, unroll=share <= 4)
        attended = rows_ref[rows, :].reshape(share, 2, row_tokens, width)
        for i in range(2):
            made[i, c] = attended[:, i].astype(BF16)
        made_copy(0, c).start()
        made_copy(2, c).start()

        @pl.when(across == 0)
        def _():
            made_copy(3, c).start()

        @pl.when(across == 0)
        def _():
            near_rows[1, c, y] = made[core, c]
            near_rows[peer_slot, c, y] = made[1 - core, c]

        @pl.when(across == 1)
        def _():
            near_rows[far_slot, c, y] = made[1 - core, c]

    attend_chunk(attend_order(0))
    queries(attend_order(1))
    attend_chunk(attend_order(1))

    loads[2].wait()
    loads[3].wait()

    def widen(even, odd):
        column = lax.rem(lax.broadcasted_iota(jnp.int32, even.shape, 0), row_tokens)
        odd_left = jnp.where(column == 0, 0.0, pltpu.roll(odd, 1, 0))
        even_right = jnp.where(column == row_tokens - 1, 0.0, pltpu.roll(even, CHUNK - 1, 0))
        return [x.astype(BF16) for x in (odd_left, even, odd, even_right)]

    valid = valid_ref[me]
    valid_above = jnp.where(me > 0, valid_ref[jnp.maximum(me - 1, 0)], 0)
    valid_below = jnp.where(me < n - 1, valid_ref[jnp.minimum(me + 1, n - 1)], 0)
    valid_rows = valid * row_tokens

    outer = across == 0
    half = 2 * channels
    limits = (valid_above, valid, valid, valid_below)

    def frames_here():
        row = lax.broadcasted_iota(jnp.int32, (CHUNK, channels), 0)
        step = lax.div(row, row_tokens)
        return lax.rem(step, share), lax.div(step, share)

    def chunk_frames(c):
        k, column = frames_here()
        return frame_of(c * share + k, column)

    def place_line(p, line, frame, limit):
        live = frame < limit
        even = jnp.where(live, line[:, :channels], 0.0)
        odd = jnp.where(live, line[:, channels:], 0.0)
        for i, part in enumerate(widen(even, odd)):
            cells[p, :, i * channels : (i + 1) * channels] = part

    def out_pixels(c, b):
        return pl.ds(c * 2 * CHUNK + b, CHUNK, 2)

    def gather_stats(c, r, results, live):
        eights = [x.reshape(CHUNK // 8, 8, channels).sum(axis=0) for x in results]
        total = jnp.sum(eights[0] + eights[1], axis=0, keepdims=True)
        size = jnp.clip(valid_rows - c * CHUNK, 0, CHUNK) * 2
        centre = total / jnp.maximum(size, 1).astype(F32)
        square = jnp.zeros((8, channels), F32)
        for x in results:
            off = jnp.where(live, x - centre, 0.0)
            square += (off * off).reshape(CHUNK // 8, 8, channels).sum(axis=0)
        square = jnp.sum(square, axis=0, keepdims=True)
        line = lax.broadcasted_iota(jnp.int32, (8, channels), 0)
        stat_acc[2 * c + r] = jnp.where(
            line == 0, total, jnp.where(line == 1, square, size.astype(F32))
        )

    def relay(c):
        near_arrival(1, c, 1 - y).wait_recv()
        relay_copy(c).start()

    def decode(c, defer):
        @pl.when(jnp.logical_not(outer))
        def _():
            near_arrival(1, c, y).wait_recv()
            near_arrival(peer_slot, c, y).wait_recv()
            near_arrival(far_slot, c, 1 - y).wait_recv()

        if not defer:

            @pl.when(jnp.logical_and(outer, exists))
            def _():
                near_arrival(far_slot, c, y).wait_recv()
                near_arrival(far_slot, c, 1 - y).wait_recv()

        frame = chunk_frames(c)
        own = jnp.dot(flat(near_rows[1, c]), outw_ref[...], preferred_element_type=F32)
        place_line(1, own[:, :half], frame, valid)
        place_line(2, own[:, half:], frame, valid)
        near_arrival(peer_slot, c, 1 - y).wait_recv()
        absent = outer if defer else jnp.logical_and(outer, jnp.logical_not(exists))
        for p, slot, low in ((0, 0, half), (3, 2, 0)):
            missing = jnp.logical_and(absent, far_slot == slot)

            @pl.when(missing)
            def _():
                cells[p] = jnp.zeros(cells.shape[1:], BF16)

            @pl.when(jnp.logical_not(missing))
            def _():
                line = jnp.dot(
                    flat(near_rows[slot, c]),
                    outw_ref[:, low : low + half],
                    preferred_element_type=F32,
                )
                place_line(p, line, frame, limits[p])

        live = frame < valid
        for r in range(2):
            results = []
            for b in range(2):
                lanes = slice(b * channels, b * channels + reach)
                result = sum(
                    jnp.dot(cells[r + d, :, lanes], convw_ref[d], preferred_element_type=F32)
                    for d in range(3)
                )
                result = jnp.where(live, result, 0.0)
                results.append(result)
                for h in range(0, channels, 128):
                    out_buf[r, h // 128, out_pixels(c, b), :] = result[:, h : h + 128]
            gather_stats(c, r, results, live)

    def finish(c):
        near_arrival(far_slot, c, y).wait_recv()
        near_arrival(far_slot, c, 1 - y).wait_recv()
        frame = chunk_frames(c)
        line = jnp.dot(
            flat(near_rows[far_slot, c]),
            outw_ref[:, pl.ds(pl.multiple_of((1 - core) * half, half), half)],
            preferred_element_type=F32,
        )
        place_line(0, line, frame, jnp.where(core == 0, valid_above, valid_below))
        live = frame < valid
        results = []
        for b in range(2):
            lanes = slice(b * channels, b * channels + reach)
            result = jnp.dot(cells[0, :, lanes], convw_ref[far_slot], preferred_element_type=F32)
            before = jnp.concatenate(
                [out_buf[core, h, out_pixels(c, b), :] for h in range(channels // 128)], axis=1
            )
            result = before + jnp.where(live, result, 0.0)
            results.append(result)
            for h in range(0, channels, 128):
                out_buf[core, h // 128, out_pixels(c, b), :] = result[:, h : h + 128]
        gather_stats(c, core, results, live)

    def reach_beyond(*steps):
        @pl.when(exists)
        def _():
            for k in steps:
                made_copy(1, attend_order(k)).start()

    def first_decode():
        decode(attend_order(0), True)

    @pl.when(jnp.logical_and(inner, core == 1))
    def _():
        reach_beyond(0, 1)
        relay(attend_order(0))
        first_decode()

    @pl.when(jnp.logical_not(inner))
    def _():
        relay(attend_order(0))

    queries(attend_order(2))
    attend_chunk(attend_order(2))

    @pl.when(jnp.logical_not(jnp.logical_and(inner, core == 1)))
    def _():
        reach_beyond(0, 1)

    @pl.when(jnp.logical_not(inner))
    def _():
        first_decode()

    queries(attend_order(3))
    attend_chunk(attend_order(3))
    reach_beyond(2, 3)

    @pl.when(jnp.logical_and(inner, core == 0))
    def _():
        relay(attend_order(0))
        first_decode()

    relay(attend_order(1))

    decode(attend_order(1), True)
    relay(attend_order(2))
    decode(attend_order(2), True)

    @pl.when(jnp.logical_and(outer, exists))
    def _():
        finish(attend_order(0))

    relay(attend_order(3))

    @pl.when(jnp.logical_and(outer, exists))
    def _():
        @pl.loop(1, 3)
        def _(k):
            finish(attend_order(k))

    decode(attend_order(3), False)

    group_row = lax.broadcasted_iota(jnp.int32, (channels, channels), 0) // group_size
    group_col = lax.broadcasted_iota(jnp.int32, (channels, channels), 1) // group_size
    group_ones = jnp.where(group_row == group_col, 1.0, 0.0).astype(BF16)

    def group_total(sums):
        parts = []
        for _ in range(3):
            part = sums.astype(BF16)
            parts.append(part)
            sums = sums - part.astype(F32)
        line = lax.broadcasted_iota(jnp.int32, (16, channels), 0)
        stacked = jnp.zeros((16, channels), F32)
        for i, part in enumerate(parts):
            stacked = jnp.where(line == i, part.astype(F32), stacked)
        found = jnp.dot(stacked.astype(BF16), group_ones, preferred_element_type=F32)
        return found[0:1] + found[1:2] + found[2:3]

    def combine(total, square, size):
        whole = jnp.sum(size, axis=0, keepdims=True)
        mean = jnp.sum(total, axis=0, keepdims=True) / whole
        off = total / jnp.maximum(size, 1.0) - mean
        return mean, jnp.sum(square + size * (off * off), axis=0, keepdims=True), whole

    mean, square, whole = combine(*[stat_acc[:, i, :] for i in range(3)])
    halves = channels // 128
    line = lax.broadcasted_iota(jnp.int32, (8, 128), 0)
    packed = jnp.zeros((8, 128), F32)
    for i, field in enumerate((mean * whole, square, whole)):
        for h in range(halves):
            packed = jnp.where(line == i * halves + h, field[:, h * 128 : (h + 1) * 128], packed)
    sent_stat[...] = packed

    @pl.loop(1, n)
    def _(s):
        stat_copy(s + (1 - side) * (n - 2 * s)).start()

    all_stat[me] = sent_stat[...]

    @pl.loop(0, n // 2)
    def _(slot):
        @pl.when(slot != mine)
        def _():
            tok_copy(slot).wait_send()

    @pl.loop(0, chunks)
    def _(c):
        made_copy(0, c).wait_send()
        made_copy(2, c).wait_send()
        relay_copy(c).wait_send()

        @pl.when(across == 0)
        def _():
            made_copy(3, c).wait_send()

        @pl.when(exists)
        def _():
            made_copy(1, c).wait_send()

    @pl.loop(1, levels)
    def _(k):
        column_copy(k).wait_send()

    @pl.loop(0, levels)
    def _(k):
        row_pass(k).wait_send()
        core_pass(k, 0).wait_send()
        core_pass(k, 1).wait_send()

    @pl.loop(1, n)
    def _(s):
        stat_copy(s).wait_recv()

    mean, square, whole = combine(
        *[
            jnp.concatenate([all_stat[:, i * halves + h, :] for h in range(halves)], axis=1)
            for i in range(3)
        ]
    )
    group_mean = group_total(mean) / group_size
    off = mean - group_mean
    group_square = group_total(square + whole * (off * off))
    mean = group_mean
    scale = gain_ref[...] * lax.rsqrt(group_square / (whole * group_size) + 1e-05)
    sides = [(r, h) for r in range(2) for h in range(channels // 128)]
    half_scale = 0.5 * scale
    half_shift = 0.5 * (bias_ref[...] - mean * scale)

    @pl.loop(0, n)
    def _(s):
        pixels = pl.ds(pl.multiple_of(s * 2 * row_tokens, 8), 2 * row_tokens)
        step = lax.rem(s, 2 * share)
        f = frame_of(lax.div(s, 2 * share) * share + lax.rem(step, share), lax.div(step, share))
        live = f < valid
        for r, h in sides:
            lanes = slice(h * 128, (h + 1) * 128)
            normed = out_buf[r, h, pixels, :] * half_scale[:, lanes] + half_shift[:, lanes]
            silu = normed + normed * jnp.tanh(normed)
            decoded_ref[f, r, :, lanes] = jnp.where(live, silu, 0.0).astype(BF16)

    @pl.loop(1, n)
    def _(s):
        stat_copy(s).wait_send()


def local(
    tokens,
    qkv_weight,
    out_weight,
    conv_weight,
    norm_gain,
    norm_bias,
    group_map,
    token_order,
    valid_frames,
):
    n = lax.axis_size("tm")
    count, width = tokens.shape
    channels = conv_weight.shape[3]
    row_tokens = count // n
    chunks = count // CHUNK
    share = n // (2 * chunks)
    state_shape = (width // 128 * (width // HEADS) + 16, 128)
    anywhere = pl.BlockSpec(memory_space=pltpu.HBM)
    vmem = pl.BlockSpec(memory_space=pltpu.VMEM)
    smem = pl.BlockSpec(memory_space=pltpu.SMEM)
    dma = pltpu.SemaphoreType.DMA
    return pl.pallas_call(
        functools.partial(mega, n),
        out_shape=pltpu.VMEM((n, 2, 2 * row_tokens, channels), BF16),
        in_specs=[anywhere] * 4 + [vmem, vmem, smem, vmem, smem],
        out_specs=vmem,
        scratch_shapes=[
            pltpu.VMEM((count, width), BF16),
            pltpu.VMEM((width, 3 * width), BF16),
            pltpu.VMEM((width, 4 * channels), BF16),
            pltpu.VMEM((3, 3 * channels, channels), BF16),
            pltpu.VMEM((n // 2, 2 * row_tokens, width), BF16),
            pltpu.VMEM((n // 2, 2 * row_tokens, width), BF16),
            pltpu.VMEM((width // BLOCK, BLOCK, BLOCK), F32),
            pltpu.VMEM((8, width), F32),
            pltpu.VMEM(state_shape, BF16),
            pltpu.VMEM((n,) + state_shape, BF16),
            pltpu.VMEM((n,) + state_shape, F32),
            pltpu.VMEM(state_shape, F32),
            pltpu.VMEM(state_shape, F32),
            pltpu.VMEM((count, width), F32),
            pltpu.VMEM((2, chunks, share, row_tokens, width), BF16),
            pltpu.VMEM((3, chunks, 2, share, row_tokens, width), BF16),
            pltpu.VMEM((4, CHUNK, 4 * channels), BF16),
            pltpu.VMEM((2 * chunks, 8, channels), F32),
            pltpu.VMEM((8, 128), F32),
            pltpu.VMEM((n, 8, 128), F32),
            pltpu.VMEM((2, channels // 128, 2 * count, 128), F32),
            dma((4,)),
            dma((n // 2,)),
            dma((n // 2,)),
            dma((2, n // 4)),
            dma((2, n // 4)),
            dma((n // 4,)),
            dma((n // 4,)),
            dma((n // 4,)),
            dma((n // 4,)),
            dma((4, chunks)),
            dma((chunks,)),
            dma((3, chunks, 2)),
            dma((n,)),
            dma((n,)),
        ],
        compiler_params=pltpu.CompilerParams(
            collective_id=0, has_side_effects=True, vmem_limit_bytes=VMEM - 2 * count * 4 * channels
        ),
    )(
        tokens,
        qkv_weight,
        out_weight,
        conv_weight.reshape(3, 3 * channels, channels),
        norm_gain[None],
        norm_bias[None],
        group_map,
        token_order[None],
        valid_frames,
    )


def solution(mesh):
    in_specs = (P(("clip", "tm"), None), P(), P(), P(), P(), P(), P("clip"), P("clip"), P("clip"))
    out_specs = P("clip", "tm", None, None)
    return jax.shard_map(local, mesh=mesh, in_specs=in_specs, out_specs=out_specs, check_vma=False)
```
